128 devices in a mesh: ax: 16 (over x, y), xs: 8 (over z, core).
Axes of the slice: x: 4, y: 4, z: 4, core: 2. Of those that a mesh axis runs over, the one named last changes fastest.
Arguments:
- state: float32 [5, 128, 128, 128], P(None, 'ax', 'xs'), may hold values from -0.2 to 6, as said below
- wall_code: int32 [128, 4, 128], replicated, may hold values from 0 to 3
Outputs:
- relaxed: float32 [5, 128, 128, 128], P(None, 'ax', 'xs')
The draws below stay inside these ranges and needn't reach their ends.
Inputs may be any that keep to these rules, and one draw needn't show every extreme that they name: `state`: components are density, axial, y and z momentum, total energy; density and pressure are positive. wall_code[i, k, j] is the type of the wall face of side k (0: y index 0, 1: y index 127, 2: z index 0, 3: z index 127) at axial cell i and transverse cell j: 0 wall, 1 evaporator, 2 condenser, 3 adiabatic wick.
All inputs are finite; a program needn't handle non-finite values.
Results may differ from the reference program's by a relative error of at most 0.00002.
Values sent between devices are 32-bit elements; how exact they have to be, the bound alone decides.
No kernel may reach another device: no remote copies, remote signals or barrier semaphores. Data moves between devices by JAX's collectives and lax.ppermute only.
A program may use at most 192 MiB of HBM per device.

```python
import jax
import jax.numpy as jnp
from jax import lax

NS = 128
NA = 128


def draw_state(key, part):
    key_list = jax.random.split(key, 7)
    grid_shape = (NA, NS, NS)
    density = jax.random.uniform(key_list[0], grid_shape, jnp.float32, 0.8, 1.2)
    axial_speed = jax.random.uniform(key_list[1], grid_shape, jnp.float32, 0.2, 0.8)
    cross_speed = jax.random.uniform(key_list[2], grid_shape, jnp.float32, -0.15, 0.15)
    depth_speed = jax.random.uniform(key_list[3], grid_shape, jnp.float32, -0.15, 0.15)
    pressure = jax.random.uniform(key_list[4], grid_shape, jnp.float32, 0.6, 0.9)
    hot_cell = jax.random.randint(key_list[5], grid_shape, 0, 16) == 0
    hot_factor = jax.random.uniform(key_list[6], grid_shape, jnp.float32, 1.5, 2.0)
    pressure = pressure * jnp.where(hot_cell, hot_factor, 1.0)
    energy = pressure / 0.4 + 0.5 * density * (axial_speed * axial_speed + cross_speed * cross_speed + depth_speed * depth_speed)
    return jnp.stack([density, density * axial_speed, density * cross_speed, density * depth_speed, energy]).astype(jnp.float32)


def with_ends(drawn, key, smallest, high):
    longest = drawn.shape.index(max(drawn.shape))
    spots = []
    for shift in (0, 1):
        where = [jax.random.randint(jax.random.fold_in(key, axis), (), 0, length) for axis, length in enumerate(drawn.shape)]
        where[longest] = (where[longest] + shift) % drawn.shape[longest]
        spots.append(tuple(where))
    return drawn.at[spots[0]].set(smallest).at[spots[1]].set(high)


def setup_inputs(seed: int = 0) -> dict:
    key_of = jax.random.split(jax.random.key(seed), 3)
    return {
        "state": draw_state(jax.random.fold_in(key_of[2], 71), 0),
        "wall_code": with_ends(jax.random.randint(key_of[1], (NA, 4, NS), 0, 4), jax.random.fold_in(key_of[1], 1), 0, 3).astype(jnp.int32),
    }


HEAT_RATIO = 1.4
CFL_NUMBER = 0.8
SECOND_COEF = 0.25
FOURTH_COEF = 0.0625
INFLOW_ENTHALPY = 3.0
WALL_STRENGTH = 0.5
SEGMENT_WEIGHTS = (0.25, 1.0 / 3.0, 0.5, 1.0)

def mirror_index(cells, extent):
    return jnp.where(cells < 0, -1 - cells, jnp.where(cells >= extent, 2 * extent - 1 - cells, cells)).astype(jnp.int32)

def reflect_signs(component):
    return jnp.where(jnp.arange(5, dtype=jnp.int32) == component, -1.0, 1.0).astype(jnp.float32).reshape(5, 1, 1, 1)

def take_cells(values, begin_at, amount, direction):
    return lax.slice_in_dim(values, begin_at, begin_at + amount, axis=direction)

def pad_mirror(values, margin, direction, component):
    extent = values.shape[direction]
    reflect = reflect_signs(component)
    lower_ghost = jnp.flip(take_cells(values, 0, margin, direction), direction) * reflect
    upper_ghost = jnp.flip(take_cells(values, extent - margin, margin, direction), direction) * reflect
    return jnp.concatenate([lower_ghost, values, upper_ghost], axis=direction)

def pressure_of(conserved):
    kinetic = 0.5 * (conserved[1] * conserved[1] + conserved[2] * conserved[2] + conserved[3] * conserved[3]) / conserved[0]
    return (HEAT_RATIO - 1.0) * (conserved[4] - kinetic)

def spectral(conserved):
    pressure = pressure_of(conserved)
    sound_speed = jnp.sqrt(HEAT_RATIO * pressure / conserved[0])
    return (jnp.abs(conserved[1]) + jnp.abs(conserved[2]) + jnp.abs(conserved[3])) / conserved[0] + 3.0 * sound_speed

def direction_terms(conserved, pressure, direction):
    component = direction + 1
    faces = pressure.shape[direction] - 3
    density = conserved[0]
    velocity = conserved[component] / density
    sound_speed = jnp.sqrt(HEAT_RATIO * pressure / density)
    wave_speed = jnp.abs(velocity) + sound_speed
    zeros = jnp.zeros_like(pressure)
    pressure_part = jnp.stack([zeros] + [pressure if entry == component else zeros for entry in (1, 2, 3)] + [pressure * velocity])
    fluxes = conserved * velocity[None] + pressure_part
    behind, centre, ahead, beyond = [take_cells(conserved, offset, faces, component) for offset in range(4)]
    press_back, press_here, press_next, press_far = [take_cells(pressure, offset, faces, direction) for offset in range(4)]
    sensor_here = jnp.abs(press_next - 2.0 * press_here + press_back) / (press_next + 2.0 * press_here + press_back)
    sensor_next = jnp.abs(press_far - 2.0 * press_next + press_here) / (press_far + 2.0 * press_next + press_here)
    second = SECOND_COEF * jnp.maximum(sensor_here, sensor_next)
    fourth = jnp.maximum(FOURTH_COEF - second, 0.0)
    face_rate = 0.5 * (take_cells(wave_speed, 1, faces, direction) + take_cells(wave_speed, 2, faces, direction))
    damping = face_rate[None] * (second[None] * (ahead - centre) - fourth[None] * (beyond - 3.0 * ahead + 3.0 * centre - behind))
    face_flux = 0.5 * (take_cells(fluxes, 1, faces, component) + take_cells(fluxes, 2, faces, component)) - damping
    return take_cells(face_flux, 1, faces - 1, component) - take_cells(face_flux, 0, faces - 1, component)

def residual_core(extended, fields, spacing):
    padded = pad_mirror(extended, 2, 3, 3)
    pressure = pressure_of(padded)
    along_axial = direction_terms(padded[:, :, 2:-2, 2:-2], pressure[:, 2:-2, 2:-2], 0)
    along_cross = direction_terms(padded[:, 2:-2, :, 2:-2], pressure[2:-2, :, 2:-2], 1)
    along_depth = direction_terms(padded[:, 2:-2, 2:-2, :], pressure[2:-2, 2:-2, :], 2)
    interior = padded[:, 2:-2, 2:-2, 2:-2]
    evaporation = fields[0]
    zeros = jnp.zeros_like(evaporation)
    gained = jnp.stack([evaporation, zeros, zeros, zeros, INFLOW_ENTHALPY * evaporation])
    moving = jnp.array([0.0, 1.0, 1.0, 1.0, 0.0], jnp.float32).reshape(5, 1, 1, 1)
    removed = fields[1][None] * interior + fields[2][None] * moving * interior
    return spacing * spacing * (along_axial + along_cross + along_depth - gained + removed)

def wall_fields(wall_code, axial_cells, cross_cells, coarse_factor, axial_extent, cross_extent):
    row_index = mirror_index(axial_cells, axial_extent)
    row_count = row_index.shape[0]
    fine_rows = (row_index[:, None] * coarse_factor + jnp.arange(coarse_factor, dtype=jnp.int32)[None, :]).reshape(-1)
    picked = jnp.take(wall_code, fine_rows, axis=0)
    strengths = jnp.stack([picked == 1, picked == 2, picked == 0]).astype(jnp.float32) * WALL_STRENGTH
    side_maps = strengths.reshape(3, row_count, coarse_factor, 4, cross_extent, coarse_factor).mean(axis=(2, 5))
    col_index = mirror_index(cross_cells, cross_extent)
    near_side = jnp.take(side_maps[:, :, 2], col_index, axis=2)
    far_side = jnp.take(side_maps[:, :, 3], col_index, axis=2)
    depth_index = jnp.arange(cross_extent, dtype=jnp.int32)
    low_wall = (col_index == 0).astype(jnp.float32)
    high_wall = (col_index == cross_extent - 1).astype(jnp.float32)
    low_depth = (depth_index == 0).astype(jnp.float32)
    high_depth = (depth_index == cross_extent - 1).astype(jnp.float32)
    return side_maps[:, :, 0][:, :, None, :] * low_wall[None, None, :, None] + side_maps[:, :, 1][:, :, None, :] * high_wall[None, None, :, None] + near_side[:, :, :, None] * low_depth[None, None, None, :] + far_side[:, :, :, None] * high_depth[None, None, None, :]

def restrict_mean(values):
    axial_len, cross_len, depth_len = values.shape[1:]
    return values.reshape(5, axial_len // 2, 2, cross_len // 2, 2, depth_len // 2, 2).mean(axis=(2, 4, 6))

def restrict_sum(values):
    axial_len, cross_len, depth_len = values.shape[1:]
    return values.reshape(5, axial_len // 2, 2, cross_len // 2, 2, depth_len // 2, 2).sum(axis=(2, 4, 6))

def prolong(values):
    return jnp.repeat(jnp.repeat(jnp.repeat(values, 2, axis=1), 2, axis=2), 2, axis=3)

def evaluate(values, fields, spacing):
    extended = pad_mirror(pad_mirror(values, 2, 1, 1), 2, 2, 2)
    return residual_core(extended, fields, spacing)

def relax(values, forcing, fields, spacing):
    factor = CFL_NUMBER / (spacing * spacing * spectral(values))
    current = values
    for segment_weight in SEGMENT_WEIGHTS:
        change = evaluate(current, fields, spacing)
        if forcing is not None:
            change = change + forcing
        current = values - segment_weight * factor[None] * change
    return current

def level_fields(wall_code, coarse_factor):
    axial_extent = NA // coarse_factor
    cross_extent = NS // coarse_factor
    return wall_fields(wall_code, jnp.arange(axial_extent, dtype=jnp.int32), jnp.arange(cross_extent, dtype=jnp.int32), coarse_factor, axial_extent, cross_extent)

def reference(state, wall_code):
    fine_fields = level_fields(wall_code, 1)
    middle_fields = level_fields(wall_code, 2)
    coarse_fields = level_fields(wall_code, 4)
    smoothed = relax(state, None, fine_fields, 1.0)
    fine_residual = evaluate(smoothed, fine_fields, 1.0)
    middle = restrict_mean(smoothed)
    middle_force = restrict_sum(fine_residual) - evaluate(middle, middle_fields, 2.0)
    middle_smooth = relax(middle, middle_force, middle_fields, 2.0)
    middle_residual = evaluate(middle_smooth, middle_fields, 2.0) + middle_force
    coarse = restrict_mean(middle_smooth)
    coarse_force = restrict_sum(middle_residual) - evaluate(coarse, coarse_fields, 4.0)
    coarse_smooth = relax(coarse, coarse_force, coarse_fields, 4.0)
    middle_new = middle_smooth + prolong(coarse_smooth - coarse)
    fine_new = smoothed + prolong(middle_new - middle)
    return relax(fine_new, None, fine_fields, 1.0)
```

```python
import functools

import jax
import jax.numpy as jnp
from jax import lax
from jax.experimental import pallas as pl
from jax.experimental.pallas import tpu as pltpu
from jax.sharding import PartitionSpec as P

HEAT_RATIO = 1.4
CFL_NUMBER = 0.8
SECOND_COEF = 0.25
FOURTH_COEF = 0.0625
INFLOW_ENTHALPY = 3.0
SEGMENT_WEIGHTS = (0.25, 1.0 / 3.0, 0.5, 1.0)
LANES = 128
EXACT = lax.Precision.HIGHEST
INTERPRET = False


def up(x, axis):
    return pltpu.roll(x, x.shape[axis] - 1, axis)


def down(x, axis):
    return pltpu.roll(x, 1, axis)


def primitives(v):
    inv = 1.0 / v[0]
    kinetic = 0.5 * (v[1] * v[1] + v[2] * v[2] + v[3] * v[3]) * inv
    pressure = (HEAT_RATIO - 1.0) * (v[4] - kinetic)
    sound = jnp.sqrt(HEAT_RATIO * pressure * inv)
    return inv, pressure, sound


def fluxes(v, q, pressure, d):
    out = [v[d], v[1] * q, v[2] * q, v[3] * q, (v[4] + pressure) * q]
    out[d] = out[d] + pressure
    return out


def sensor(back, here, ahead):
    outer = ahead + back
    twice = here + here
    return jnp.abs(outer - twice) / (outer + twice)


def weights(nu, lam):
    e2 = SECOND_COEF * nu
    e4 = jnp.maximum(FOURTH_COEF - e2, 0.0)
    k4 = lam * e4
    return lam * e2 + (k4 + k4), k4


def depth_matrix(depth):
    a = lax.broadcasted_iota(jnp.int32, (LANES, LANES), 0)
    b = lax.broadcasted_iota(jnp.int32, (LANES, LANES), 1)

    def at(by):
        return jnp.where(a == mirror(b + by, depth), 1.0, 0.0)

    above = at(1)
    half = jnp.concatenate([above, at(2) - above + at(0) - at(-1)], axis=1)
    return jnp.concatenate([half, half], axis=0).astype(jnp.bfloat16)


EVEN = (0, 1, 2, 4)


def depth_shifts(rows, matrix, depth):
    x = jnp.concatenate([v[c] for v in rows for c in EVEN], axis=0)
    if depth < LANES:
        x = jnp.where(lax.broadcasted_iota(jnp.int32, x.shape, 1) < depth, x, 0.0)
    high = x.astype(jnp.bfloat16)
    low = (x - high.astype(jnp.float32)).astype(jnp.bfloat16)
    moved = jnp.dot(
        jnp.concatenate([high, low], axis=1), matrix[...], preferred_element_type=jnp.float32
    )
    n = rows[0][0].shape[0]
    out = []
    for k in range(len(rows)):
        at = [(4 * k + m) * n for m in range(4)]
        out.append(
            {c: (moved[i : i + n, :LANES], moved[i : i + n, LANES:]) for c, i in zip(EVEN, at)}
        )
    return out


def depth_terms(v, inv, pressure, sound, depth, moved):
    lane = lax.broadcasted_iota(jnp.int32, pressure.shape, 1)
    lo, hi, outside = lane == 0, lane == depth - 1, lane >= depth - 1
    q = v[3] * inv
    q_up = jnp.where(hi, -q, up(q, 1))
    p_up = jnp.where(hi, pressure, up(pressure, 1))
    p_dn = jnp.where(lo, pressure, down(pressure, 1))
    wave = jnp.abs(q) + sound
    wave_up = jnp.abs(q_up) + jnp.where(hi, sound, up(sound, 1))
    nu = sensor(p_dn, pressure, p_up)
    k2, k4 = weights(jnp.maximum(nu, jnp.where(hi, nu, up(nu, 1))), wave + wave_up)
    d1 = jnp.where(hi, -v[3], up(v[3], 1)) - v[3]
    d1_dn = jnp.where(lo, v[3] + v[3], down(d1, 1))
    d1_up = jnp.where(hi, d1_dn, up(d1, 1))
    above = {c: x[0] for c, x in moved.items()}
    above[3] = d1 + v[3]
    flux = fluxes(v, q, pressure, 3)
    flux_up = fluxes(above, q_up, p_up, 3)
    out = []
    for c in range(5):
        if c == 3:
            g = (flux[c] + flux_up[c]) - (k2 * d1 - k4 * (d1_up + d1_dn))
            w2, w4 = weights(nu, wave + wave)
            wall = (flux[c] + flux[c]) - (w2 * (v[c] + v[c]) - w4 * (d1 + d1))
            out.append(g - jnp.where(lo, wall, down(g, 1)))
        else:
            g = (flux[c] + flux_up[c]) - (k2 * (above[c] - v[c]) - k4 * moved[c][1])
            g = jnp.where(outside, 0.0, g)
            out.append(g - down(g, 1))
    return out


class Band:
    def __init__(self, base, count):
        self.base, self.count = base, count
        self.tall = -(-count // 8) * 8
        self.cross = -(-(count + 2) // 8) * 8
        self.cols = pl.ds(base, self.tall)


def cross_terms(w, prim, r, band, shift):
    n, base = band.cross, band.base - 1
    vm, v0, v1, v2 = [[w[c, r, pl.ds(base + k, n)] for c in range(5)] for k in (-1, 0, 1, 2)]
    pm, p0, p1 = [prim[1, r, pl.ds(base + k, n)] for k in (-1, 0, 1)]
    q = v0[2] * prim[0, r, pl.ds(base, n)]
    wave = jnp.abs(q) + prim[2, r, pl.ds(base, n)]
    nu = sensor(pm, p0, p1)
    flux = fluxes(v0, q, p0, 2)
    for k, x in enumerate([nu, wave] + flux):
        shift[k, 0:n] = x
    k2, k4 = weights(jnp.maximum(nu, shift[0, 1 : n + 1]), wave + shift[1, 1 : n + 1])
    out = []
    for c in range(5):
        side = (v2[c] - v1[c]) + (v0[c] - vm[c])
        g = (flux[c] + shift[2 + c, 1 : n + 1]) - (k2 * (v1[c] - v0[c]) - k4 * side)
        shift[7 + c, 0:n] = g
        out.append(shift[7 + c, 1 : band.tall + 1] - g[0 : band.tall])
    return out


class Level:
    def __init__(self, depth, fields, carry, shift, matrix):
        self.depth, self.fields, self.carry, self.shift = depth, fields, carry, shift
        self.matrix = matrix
        matrix[...] = depth_matrix(depth)

    def face(self, w, prim, r, band, carry):
        n, cols = band.tall, band.cols
        vm, v0, v1, v2 = [[w[c, r + k, cols] for c in range(5)] for k in (-1, 0, 1, 2)]
        p0, p1, p2 = [prim[1, r + k, cols] for k in (0, 1, 2)]
        q1 = v1[1] * prim[0, r + 1, cols]
        wave1 = jnp.abs(q1) + prim[2, r + 1, cols]
        nu1 = sensor(p0, p1, p2)
        f1 = fluxes(v1, q1, p1, 1)
        nu0 = carry[5, 0:n]
        wave0 = carry[6, 0:n]
        k2, k4 = weights(jnp.maximum(nu0, nu1), wave0 + wave1)
        g = []
        for c in range(5):
            d1 = v1[c] - v0[c]
            side = (v2[c] - v1[c]) + (v0[c] - vm[c])
            g.append((carry[7 + c, 0:n] + f1[c]) - (k2 * d1 - k4 * side))
        carry[5, 0:n] = nu1
        carry[6, 0:n] = wave1
        for c in range(5):
            carry[7 + c, 0:n] = f1[c]
        return g, v0

    def start(self, w, prim, r, band, carry):
        n, cols = band.tall, band.cols
        p = [prim[1, r + k, cols] for k in (-2, -1, 0)]
        v = [w[c, r - 1, cols] for c in range(5)]
        q = v[1] * prim[0, r - 1, cols]
        carry[5, 0:n] = sensor(*p)
        carry[6, 0:n] = jnp.abs(q) + prim[2, r - 1, cols]
        for c, f in enumerate(fluxes(v, q, p[1], 1)):
            carry[7 + c, 0:n] = f
        g, _ = self.face(w, prim, r - 1, band, carry)
        for c in range(5):
            carry[c, 0:n] = g[c]

    def rows(self, w, prim, begins, count, band, sink, unroll=2):
        for k, begin in enumerate(begins):
            self.start(w, prim, begin, band, self.carry.at[k])
        unroll = min(unroll, count)

        @pl.loop(0, count // unroll)
        def _(i):
            jobs = [(k, begin + i * unroll + u) for u in range(unroll) for k, begin in enumerate(begins)]
            vs = [[w[c, r, band.cols] for c in range(5)] for _, r in jobs]
            moved = depth_shifts(vs, self.matrix, self.depth)
            for j, (k, r) in enumerate(jobs):
                carry, shift = self.carry.at[k], self.shift.at[j]
                self.row(w, prim, r, band, sink, carry, shift, moved[j])

    def row(self, w, prim, r, band, sink, carry, shift, moved):
        fields, n, cols = self.fields, band.tall, band.cols
        g, v = self.face(w, prim, r, band, carry)
        total = [g[c] - carry[c, 0:n] for c in range(5)]
        for c in range(5):
            carry[c, 0:n] = g[c]
        part = depth_terms(
            v, prim[0, r, cols], prim[1, r, cols], prim[2, r, cols], self.depth, moved
        )
        total = [a + b for a, b in zip(total, part)]
        part = cross_terms(w, prim, r, band, shift)
        total = [a + b for a, b in zip(total, part)]
        evap = fields[0, r, cols]
        suction = fields[1, r, cols]
        both = suction + fields[2, r, cols]
        total = [
            total[0] + (suction * v[0] - evap),
            total[1] + both * v[1],
            total[2] + both * v[2],
            total[3] + both * v[3],
            total[4] + (suction * v[4] - INFLOW_ENTHALPY * evap),
        ]
        sink(r, v, total, band)


def fill_prim(w, prim, begin, end):
    @pl.loop(begin, end, unroll=4)
    def _(r):
        prim[0, r], prim[1, r], prim[2, r] = primitives([w[c, r] for c in range(5)])


def rate_row(v, pressure, sound, inv):
    wave = (jnp.abs(v[1]) + jnp.abs(v[2]) + jnp.abs(v[3])) * inv + 3.0 * sound
    return (0.5 * CFL_NUMBER) / wave


def store_row(w, prim, r, cols, new):
    for c in range(5):
        w[c, r, cols] = new[c]
    prim[0, r, cols], prim[1, r, cols], prim[2, r, cols] = primitives(new)


def flip8(x):
    sub = lax.broadcasted_iota(jnp.int32, x.shape, 0)
    for step in (1, 2, 4):
        if step == 4:
            x = pltpu.roll(x, 4, 0)
        else:
            x = jnp.where((sub & step) == 0, pltpu.roll(x, 8 - step, 0), pltpu.roll(x, step, 0))
    return x


def mirror(cell, extent):
    return jnp.where(cell < 0, -1 - cell, jnp.where(cell >= extent, 2 * extent - 1 - cell, cell))


def pick(shape, condition):
    a = lax.broadcasted_iota(jnp.int32, shape, 0)
    b = lax.broadcasted_iota(jnp.int32, shape, 1)
    return jnp.where(condition(a, b), 1.0, 0.0)


def matmul(a, b):
    return jnp.dot(a, b, precision=EXACT, preferred_element_type=jnp.float32)


def fine_window(pos, own, before, after, left, right, w, ends):
    for c in range(5):
        w[c, 0:8, 8:24] = before[c]
        w[c, 8:16, 8:24] = own[c]
        w[c, 16:24, 8:24] = after[c]
        w[c, 2:22, 0:8] = left[c]
        w[c, 2:22, 24:32] = right[c]

    def cross(at, to, source):
        @pl.when(pos[1] == at)
        def _():
            @pl.loop(2, 22)
            def _(r):
                for c in range(5):
                    x = flip8(w[c, r, source : source + 8])
                    w[c, r, to : to + 8] = -x if c == 2 else x

    cross(0, 0, 8)
    cross(ends[1] - 1, 24, 16)

    def axial(at, to, source, step):
        @pl.when(pos[0] == at)
        def _():
            @pl.loop(0, 8)
            def _(k):
                for c in range(5):
                    x = w[c, source + step * k, 0:32]
                    w[c, to - step * k, 0:32] = -x if c == 1 else x

    axial(0, 7, 8, 1)
    axial(ends[0] - 1, 16, 15, -1)


FINE_PLAN = (
    (((6,), 12, Band(2, 28)), ((2, 18), 4, Band(6, 20))),
    (((6,), 12, Band(4, 24)), ((4, 18), 2, Band(8, 16))),
    (((8,), 8, Band(6, 20)), ((6, 16), 2, Band(8, 16))),
    (((8,), 8, Band(8, 16)),),
)


def fine_relax_kernel(
    ends, pos, own, before, after, left, right, fields, out, *rest
):
    slabs, (wa, wb, wc, prim_a, prim_b, rate, carry, shift, matrix) = rest[:-9], rest[-9:]
    fine_window(pos, own, before, after, left, right, wa, ends)
    fill_prim(wa, prim_a, 0, 24)

    @pl.loop(2, 22, unroll=4)
    def _(r):
        rate[r] = rate_row([wa[c, r] for c in range(5)], prim_a[1, r], prim_a[2, r], prim_a[0, r])

    level = Level(LANES, fields, carry, shift, matrix)
    source, source_prim = wa, prim_a
    for k, weight in enumerate(SEGMENT_WEIGHTS):
        last = k == 3
        target = (wb, wc, wb, None)[k]
        target_prim = (prim_b, prim_a, prim_b, None)[k]

        def sink(r, v, total, band, weight=weight, last=last, target=target, prim=target_prim):
            cols = band.cols
            scale = weight * rate[r, cols]
            new = [wa[c, r, cols] - scale * total[c] for c in range(5)]
            if last:
                for c in range(5):
                    out[c, r - 8] = new[c]
                    if slabs:
                        slabs[2][c, r - 8] = new[c][14:16]
                        slabs[3][c, r - 8] = new[c][0:2]
            else:
                store_row(target, prim, r, cols, new)

        for begins, count, band in FINE_PLAN[k]:
            level.rows(source, source_prim, begins, count, band, sink)
        source, source_prim = target, target_prim
    if slabs:
        for c in range(5):
            for k in range(2):
                slabs[0][c, k] = out[c, 6 + k]
                slabs[1][c, k] = out[c, k]


def vmem(*shape):
    return pltpu.VMEM(shape, jnp.float32)


def call(kernel, out_shapes, scratch, flops, *args):
    specs = [pl.BlockSpec(memory_space=pltpu.SMEM)]
    specs += [pl.BlockSpec(memory_space=pltpu.VMEM)] * (len(args) - 1)
    single = len(out_shapes) == 1
    outs = [jax.ShapeDtypeStruct(s, jnp.float32) for s in out_shapes]
    out_specs = [pl.BlockSpec(memory_space=pltpu.VMEM)] * len(outs)
    moved = sum(4 * a.size for a in args) + sum(4 * o.size for o in outs)
    return pl.pallas_call(
        kernel,
        out_shape=outs[0] if single else outs,
        in_specs=specs,
        out_specs=out_specs[0] if single else out_specs,
        scratch_shapes=scratch,
        cost_estimate=pl.CostEstimate(flops=flops, bytes_accessed=moved, transcendentals=0),
        interpret=INTERPRET,
    )(*args)


MATRIX = pltpu.VMEM((2 * LANES, 2 * LANES), jnp.bfloat16)
FINE_COLS = 40
MIDDLE_COLS = 32
COARSE_COLS = 24


def fine_relax(ends, pos, own, halos, fields, slabs):
    scratch = [vmem(5, 24, FINE_COLS, LANES)] * 3 + [vmem(3, 24, FINE_COLS, LANES)] * 2
    scratch += [vmem(24, FINE_COLS, LANES), vmem(2, 12, 32, LANES), vmem(4, 12, 40, LANES), MATRIX]
    outs = [own.shape]
    if slabs:
        outs += [(5, 2, 16, LANES)] * 2 + [(5, 8, 2, LANES)] * 2
    return call(
        functools.partial(fine_relax_kernel, ends),
        outs,
        scratch,
        80_000_000,
        pos,
        own,
        *halos,
        fields,
    )


def restrict_rows(ref, scratch, rows, count):
    parts = []
    for c in range(5):
        for r in range(rows // 2):
            scratch[0:count] = ref[c, 2 * r] + ref[c, 2 * r + 1]
            parts.append(
                scratch[pl.ds(0, count // 2, stride=2)] + scratch[pl.ds(1, count // 2, stride=2)]
            )
    return jnp.concatenate(parts, axis=0)


def fine_residual_kernel(
    ends, pos, own, before, after, left, right, fields, out, w, prim, res, carry, shift, matrix,
    pair,
):
    for c in range(5):
        w[c, 0:2, 8:24] = before[c]
        w[c, 2:10, 8:24] = own[c]
        w[c, 10:12, 8:24] = after[c]
        w[c, 2:10, 6:8] = left[c]
        w[c, 2:10, 24:26] = right[c]

    def cross(at, to, source, step):
        @pl.when(pos[1] == at)
        def _():
            for k in range(2):
                for c in range(5):
                    x = w[c, 2:10, source + step * k : source + step * k + 1]
                    w[c, 2:10, to - step * k : to - step * k + 1] = -x if c == 2 else x

    cross(0, 7, 8, 1)
    cross(ends[1] - 1, 24, 23, -1)

    def axial(at, to, source, step):
        @pl.when(pos[0] == at)
        def _():
            for k in range(2):
                for c in range(5):
                    x = w[c, source + step * k]
                    w[c, to - step * k] = -x if c == 1 else x

    axial(0, 1, 2, 1)
    axial(ends[0] - 1, 10, 9, -1)
    fill_prim(w, prim, 0, 12)

    def sink(r, v, total, band):
        for c in range(5):
            res[c, r - 2] = 0.5 * total[c]

    level = Level(LANES, ShiftedRows(fields, 6), carry, shift, matrix)
    level.rows(w, prim, (2,), 8, Band(8, 16), sink)
    low = pick((LANES, LANES), lambda a, b: a // 2 == b)
    high = pick((LANES, LANES), lambda a, b: a // 2 + 64 == b)
    packed = matmul(0.125 * restrict_rows(own, pair, 8, 16), low)
    packed = packed + matmul(restrict_rows(res, pair, 8, 16), high)
    for c in range(5):
        for r in range(4):
            at = (c * 4 + r) * 8
            out[c, r] = packed[at : at + 8]


class ShiftedRows:
    def __init__(self, ref, by):
        self.ref, self.by = ref, by

    def __getitem__(self, index):
        c, r, cols = index
        return self.ref[c, r + self.by, cols]


def fine_residual(ends, pos, own, halos, fields):
    scratch = [vmem(5, 12, FINE_COLS, LANES), vmem(3, 12, FINE_COLS, LANES)]
    scratch += [vmem(5, 8, 16, LANES), vmem(1, 12, 16, LANES), vmem(2, 12, 32, LANES), MATRIX]
    scratch += [vmem(16, LANES)]
    return call(
        functools.partial(fine_residual_kernel, ends),
        [(5, 4, 8, LANES)],
        scratch,
        8_000_000,
        pos,
        own,
        *halos,
        fields,
    )


def middle_kernel(
    ends, pos, before2, before, own, after, after2, left, right, fields, out, diff,
    v0, wa, wb, force, prim_v, prim_a, prim_b, rate, res, carry, shift, matrix, pair,
):
    for k, ref in enumerate((before2, before, own, after, after2)):
        for c in range(5):
            v0[c, 4 * k : 4 * k + 4, 8:16] = ref[c]
    for c in range(5):
        v0[c, 2:18, 0:8] = left[c]
        v0[c, 2:18, 16:24] = right[c]
    begin = 4 * pos[0] - 8
    extent = 4 * ends[0]

    @pl.when((pos[0] < 2) | (pos[0] >= ends[0] - 2))
    def _():
        @pl.loop(0, 20)
        def _(r):
            at = mirror(begin + r, extent) - begin

            @pl.when(at != r)
            def _():
                for c in range(5):
                    x = v0[c, at, 0:24]
                    v0[c, r, 0:24] = -x if c == 1 else x

    def cross(at, to, source):
        @pl.when(pos[1] == at)
        def _():
            @pl.loop(0, 20)
            def _(r):
                for c in range(5):
                    x = flip8(v0[c, r, source : source + 8])
                    v0[c, r, to : to + 8] = -x if c == 2 else x

    cross(0, 0, 8)
    cross(ends[1] - 1, 16, 8)
    level = Level(64, fields, carry, shift, matrix)
    chain(level, MIDDLE_PLAN, 4.0, 20, 24, v0, wa, wb, force, prim_v, prim_a, prim_b, rate, 64)
    inner = pl.ds(8, 8)

    def sink(r, v, total, band):
        for c in range(5):
            res[c, r - 8] = 2.0 * (total[c] + force[c, r, inner])

    level.rows(wb, prim_a, (8,), 4, Band(8, 8), sink, 4)
    valid = lax.broadcasted_iota(jnp.int32, (8, LANES), 1) < 64
    for c in range(5):
        for r in range(4):
            x = wb[c, 8 + r, inner]
            diff[c, r] = jnp.where(valid, x - v0[c, 8 + r, inner], 0.0)
            res[c, r] = jnp.where(valid, res[c, r], 0.0)
            res[5 + c, r] = jnp.where(valid, x, 0.0)
    total = None
    for k, (ref, scale) in enumerate(((res.at[pl.ds(5, 5)], 0.125), (res.at[pl.ds(0, 5)], 1.0))):
        for r in range(2):
            parts = []
            for c in range(5):
                pair[0:8] = ref[c, 2 * r] + ref[c, 2 * r + 1]
                parts.append(
                    pair[pl.ds(0, 4, stride=2)] + pair[pl.ds(1, 4, stride=2)]
                )
                parts.append(jnp.zeros((4, LANES), jnp.float32))
            shift = 64 * r + 32 * k
            m = pick((LANES, LANES), lambda a, b, s=shift: (a // 2 + s == b) & (a < 64))
            part = matmul(scale * jnp.concatenate(parts, axis=0), m)
            total = part if total is None else total + part
    for k in range(out.shape[0]):
        for c in range(5):
            out[k, c] = total[8 * c : 8 * c + 4]


MIDDLE_PLAN = (
    (((6,), 8, Band(2, 20), 2), ((2, 14), 4, Band(6, 12), 1)),
    (((6,), 8, Band(4, 16), 2), ((4, 14), 2, Band(8, 8), 2)),
    (((8,), 4, Band(6, 12), 2), ((6, 12), 2, Band(8, 8), 2)),
)
COARSE_PLAN = (
    (((6,), 2, Band(2, 12), 2), ((2, 8), 4, Band(4, 8), 2)),
    (((4,), 6, Band(4, 8), 3),),
    (((6,), 2, Band(6, 4), 2),),
)


def chain(level, plan, area, rows, cols, v0, wa, wb, force, prim_v, prim_a, prim_b, rate, half):
    @pl.loop(0, rows, unroll=2)
    def _(r):
        every = pl.ds(0, cols)
        v = [v0[c, r, every] for c in range(5)]
        inv, pressure, sound = primitives(v)
        prim_v[0, r, every], prim_v[1, r, every], prim_v[2, r, every] = inv, pressure, sound
        scale = rate_row(v, pressure, sound, inv)
        rate[r, every] = scale
        new = []
        for c in range(5):
            total = (2.0 / area) * pltpu.roll(v[c], LANES - half, 1)
            force[c, r, every] = total
            new.append(v[c] - SEGMENT_WEIGHTS[0] * scale * total)
        store_row(wa, prim_a, r, every, new)

    def force_sink(r, v, total, band):
        for c in range(5):
            force[c, r, band.cols] = force[c, r, band.cols] - total[c]

    for begins, count, band, unroll in plan[0]:
        level.rows(v0, prim_v, begins, count, band, force_sink, unroll)
    source, source_prim = wa, prim_a
    for k in (1, 2, 3):
        target = (wb, wa, wb)[k - 1]
        target_prim = (prim_b, prim_v, prim_a)[k - 1]

        def sink(r, v, total, band, k=k, target=target, prim=target_prim):
            cols = band.cols
            scale = SEGMENT_WEIGHTS[k] * rate[r, cols]
            new = [v0[c, r, cols] - scale * (total[c] + force[c, r, cols]) for c in range(5)]
            store_row(target, prim, r, cols, new)

        for begins, count, band, unroll in plan[k - 1]:
            level.rows(source, source_prim, begins, count, band, sink, unroll)
        source, source_prim = target, target_prim


def middle(ends, pos, pieces, left, right, fields):
    cols = MIDDLE_COLS
    scratch = [vmem(5, 20, cols, LANES)] * 4 + [vmem(3, 20, cols, LANES)] * 3
    scratch += [vmem(20, cols, LANES), vmem(10, 4, 8, LANES), vmem(2, 12, 24, LANES)]
    scratch += [vmem(4, 12, 32, LANES), MATRIX, vmem(8, LANES)]
    return call(
        functools.partial(middle_kernel, ends),
        [(ends[0], 5, 4, LANES), (5, 4, 8, LANES)],
        scratch,
        60_000_000,
        pos,
        *pieces,
        left,
        right,
        fields,
    )


def coarse_kernel(
    ends, pos, own, left1, left2, right1, right2, fields, diff, smoothed, out,
    raw, v0, wa, wb, force, prim_v, prim_a, prim_b, rate, carry, shift, matrix, tall,
    wide,
):
    raw[...] = jnp.zeros_like(raw)
    for k, ref in enumerate((left2, left1, own, right1, right2)):
        for c in range(5):
            for b in range(7):
                at = (c * 7 + b) * LANES
                raw[4 * k : 4 * k + 4, at : at + LANES] = ref[c, b]
    first = 4 * pos[1] - 6
    extent = 4 * ends[1]
    j = lax.broadcasted_iota(jnp.int32, (16, 24), 0)
    s = lax.broadcasted_iota(jnp.int32, (16, 24), 1)
    cell = mirror(first + j, extent)
    moved = jnp.where(s == cell - first + 2, 1.0, 0.0)
    raw[0:16] = matmul(moved, raw[...])
    row = lax.broadcasted_iota(jnp.int32, (16, LANES), 0) + first
    cross_sign = jnp.where((row < 0) | (row >= extent), -1.0, 1.0)
    begin = 2 * pos[0] - 6
    ax_extent = 2 * ends[0]
    origin = 2 * jnp.clip(pos[0] - 3, 0, ends[0] - 7)

    @pl.loop(0, 14)
    def _(r):
        g = begin + r
        at = mirror(g, ax_extent)
        sign = jnp.where(at == g, 1.0, -1.0)
        block = (at - origin) // 2
        odd = (at - origin) % 2
        for c in range(5):
            x = raw[0:16, pl.ds(pl.multiple_of((c * 7 + block) * LANES, LANES), LANES)]
            x = jnp.where(odd == 1, pltpu.roll(x, 64, 1), x)
            if c == 1:
                x = x * sign
            if c == 2:
                x = x * cross_sign
            v0[c, r, 0:16] = x

    level = Level(32, fields, carry, shift, matrix)
    chain(level, COARSE_PLAN, 16.0, 14, 16, v0, wa, wb, force, prim_v, prim_a, prim_b, rate, 32)
    lane = lax.broadcasted_iota(jnp.int32, (16, LANES), 1)
    sub = lax.broadcasted_iota(jnp.int32, (16, LANES), 0)
    valid = (lane < 32) & (sub >= 6) & (sub < 10)
    parts = []
    for c in range(5):
        for r in range(2):
            parts.append(jnp.where(valid, wb[c, 6 + r, 0:16] - v0[c, 6 + r, 0:16], 0.0))
    wide[...] = matmul(
        jnp.concatenate(parts, axis=0), pick((LANES, LANES), lambda a, b: a == b // 4)
    )
    parts = [diff[c, r] for c in range(5) for r in range(4)]
    tall[...] = matmul(
        jnp.concatenate(parts, axis=0), pick((LANES, LANES), lambda a, b: a == b // 2)
    )
    four = pick((16, 16), lambda a, b: b == 6 + a // 4)
    two = pick((16, 8), lambda a, b: b == a // 2)
    for c in range(5):
        for r in range(2):
            at = (c * 2 + r) * 16
            big = matmul(four, wide[at : at + 16])
            for m in range(2):
                at = (c * 4 + 2 * r + m) * 8
                step = big + matmul(two, tall[at : at + 8])
                for n in range(2):
                    row = 4 * r + 2 * m + n
                    out[c, row] = smoothed[c, row] + step


def coarse(ends, pos, own, neighbours, fields, diff, smoothed):
    scratch = [vmem(24, 35 * LANES)]
    cols = COARSE_COLS
    scratch += [vmem(5, 14, cols, LANES)] * 4 + [vmem(3, 14, cols, LANES)] * 3
    scratch += [vmem(14, cols, LANES), vmem(2, 12, 16, LANES), vmem(4, 12, 24, LANES), MATRIX]
    scratch += [vmem(160, LANES), vmem(160, LANES)]
    return call(
        functools.partial(coarse_kernel, ends),
        [smoothed.shape],
        scratch,
        20_000_000,
        pos,
        own,
        *neighbours,
        fields,
        diff,
        smoothed,
    )


def shifted(x, axis, by):
    size = lax.axis_size(axis)
    return lax.ppermute(x, axis, [(i, i + by) for i in range(size) if 0 <= i + by < size])


def wide_halos(own):
    before = shifted(own, "ax", 1)
    after = shifted(own, "ax", -1)

    def slab(cols):
        return jnp.concatenate([before[:, 2:, cols], own[:, :, cols], after[:, :6, cols]], axis=1)

    left = shifted(slab(slice(8, 16)), "xs", 1)
    right = shifted(slab(slice(0, 8)), "xs", -1)
    return before, after, left, right


def wall_terms_kernel(factor, rows, count, origin, ends, pos, code, out, sides):
    extent = 8 * ends[0] // factor
    depth = 16 * ends[1] // factor
    scale = 1.0 / (factor * factor)
    begin = (8 // factor) * pos[0] - origin[0]
    first = (16 // factor) * pos[1] - origin[1]
    lane = lax.broadcasted_iota(jnp.int32, (count, LANES), 1)
    cell = mirror(lax.broadcasted_iota(jnp.int32, (count, LANES), 0) + first, depth)
    kinds = (1, 2, 0)

    def counts(r, kind, side):
        g = mirror(begin + r, extent)
        total = None
        for k in range(factor):
            hit = jnp.where(code[g * factor + k, side : side + 1] == kind, 1.0, 0.0)
            total = hit if total is None else total + hit
        return total

    if factor > 1:

        @pl.loop(0, rows, unroll=2)
        def _(r):
            for t, kind in enumerate(kinds):
                for side in range(2):
                    sides[pl.ds(r * 8 + 2 * t + side, 1)] = counts(r, kind, side)
            sides[pl.ds(r * 8 + 6, 2)] = jnp.zeros((2, LANES), jnp.float32)

        gather = pick((LANES, LANES), lambda a, b: a // factor == b)
        sides[...] = matmul(sides[...], gather)

    inside = cell == lane // factor

    @pl.loop(0, rows, unroll=2)
    def _(r):
        for t, kind in enumerate(kinds):
            edge = []
            for side in range(2):
                if factor > 1:
                    edge.append(sides[pl.ds(r * 8 + 2 * t + side, 1)])
                else:
                    edge.append(counts(r, kind, side))
            for side in (2, 3):
                line = jnp.broadcast_to(counts(r, kind, side), (count, LANES))
                edge.append(jnp.sum(jnp.where(inside, line, 0.0), axis=1, keepdims=True))
            total = jnp.where(cell == 0, edge[0], 0.0) + jnp.where(cell == depth - 1, edge[1], 0.0)
            total = total + jnp.where(lane == 0, edge[2], 0.0)
            total = total + jnp.where(lane == depth - 1, edge[3], 0.0)
            out[t, r] = scale * total


def wall_terms(ends, pos, code, factor, rows, count, origin):
    return call(
        functools.partial(wall_terms_kernel, factor, rows, count, origin, ends),
        [(3, rows, count, LANES)],
        [vmem(rows * 8, LANES)],
        1_000_000,
        pos,
        code,
    )


def per_device(state, wall_code):
    ends = (lax.axis_size("ax"), lax.axis_size("xs"))
    ax, xs = lax.axis_index("ax"), lax.axis_index("xs")
    pos = jnp.stack([ax, xs]).astype(jnp.int32)
    fine_fields = wall_terms(ends, pos, wall_code, 1, 24, FINE_COLS, (8, 8))
    middle_fields = wall_terms(ends, pos, wall_code, 2, 20, MIDDLE_COLS, (8, 8))
    coarse_fields = wall_terms(ends, pos, wall_code, 4, 14, COARSE_COLS, (6, 6))

    smoothed, high, low, last, first = fine_relax(
        ends, pos, state, wide_halos(state), fine_fields, True
    )
    halos = (
        shifted(high, "ax", 1),
        shifted(low, "ax", -1),
        shifted(last, "xs", 1),
        shifted(first, "xs", -1),
    )
    packed = fine_residual(ends, pos, smoothed, halos, fine_fields)

    pieces = [shifted(packed, "ax", by) for by in (2, 1)] + [packed]
    pieces += [shifted(packed, "ax", by) for by in (-1, -2)]
    slab = jnp.concatenate(
        [pieces[0][:, 2:], pieces[1], pieces[2], pieces[3], pieces[4][:, :2]], axis=1
    )
    block, diff = middle(
        ends, pos, pieces, shifted(slab, "xs", 1), shifted(slab, "xs", -1), middle_fields
    )

    column = lax.all_to_all(block, "ax", 0, 0)
    start = jnp.clip(ax - 3, 0, ends[0] - 7)
    column = lax.dynamic_slice_in_dim(column, start, 7, axis=0)
    column = jnp.transpose(column, (1, 0, 2, 3))
    neighbours = [shifted(column, "xs", by) for by in (1, 2, -1, -2)]
    fine_new = coarse(ends, pos, column, neighbours, coarse_fields, diff, smoothed)

    return fine_relax(ends, pos, fine_new, wide_halos(fine_new), fine_fields, False)


def solution(mesh):
    in_specs = (P(None, "ax", "xs", None), P())
    out_specs = P(None, "ax", "xs", None)
    return jax.shard_map(
        per_device, mesh=mesh, in_specs=in_specs, out_specs=out_specs, check_vma=False
    )
```

```python
import functools

import jax
import jax.numpy as jnp
from jax import lax
from jax.experimental import pallas as pl
from jax.experimental.pallas import tpu as pltpu
from jax.sharding import PartitionSpec as P

HEAT_RATIO = 1.4
CFL_NUMBER = 0.8
SECOND_COEF = 0.25
FOURTH_COEF = 0.0625
INFLOW_ENTHALPY = 3.0
SEGMENT_WEIGHTS = (0.25, 1.0 / 3.0, 0.5, 1.0)
LANES = 128
EXACT = lax.Precision.HIGHEST
INTERPRET = False


def up(x, axis):
    return pltpu.roll(x, x.shape[axis] - 1, axis)


def down(x, axis):
    return pltpu.roll(x, 1, axis)


def primitives(v):
    inv = 1.0 / v[0]
    kinetic = 0.5 * (v[1] * v[1] + v[2] * v[2] + v[3] * v[3]) * inv
    pressure = (HEAT_RATIO - 1.0) * (v[4] - kinetic)
    sound = jnp.sqrt(HEAT_RATIO * pressure * inv)
    return inv, pressure, sound


def fluxes(v, q, pressure, d):
    out = [v[d], v[1] * q, v[2] * q, v[3] * q, (v[4] + pressure) * q]
    out[d] = out[d] + pressure
    return out


def sensor(back, here, ahead):
    outer = ahead + back
    twice = here + here
    return jnp.abs(outer - twice) / (outer + twice)


def weights(nu, lam):
    e2 = SECOND_COEF * nu
    e4 = jnp.maximum(FOURTH_COEF - e2, 0.0)
    k4 = lam * e4
    return lam * e2 + (k4 + k4), k4


def depth_matrix(depth):
    a = lax.broadcasted_iota(jnp.int32, (LANES, LANES), 0)
    b = lax.broadcasted_iota(jnp.int32, (LANES, LANES), 1)

    def at(by):
        return jnp.where(a == mirror(b + by, depth), 1.0, 0.0)

    above = at(1)
    half = jnp.concatenate([above, at(2) - above + at(0) - at(-1)], axis=1)
    return jnp.concatenate([half, half], axis=0).astype(jnp.bfloat16)


EVEN = (0, 1, 2, 4)


def depth_shifts(rows, matrix, depth):
    x = jnp.concatenate([v[c] for v in rows for c in EVEN], axis=0)
    if depth < LANES:
        x = jnp.where(lax.broadcasted_iota(jnp.int32, x.shape, 1) < depth, x, 0.0)
    high = x.astype(jnp.bfloat16)
    low = (x - high.astype(jnp.float32)).astype(jnp.bfloat16)
    moved = jnp.dot(
        jnp.concatenate([high, low], axis=1), matrix[...], preferred_element_type=jnp.float32
    )
    n = rows[0][0].shape[0]
    out = []
    for k in range(len(rows)):
        at = [(4 * k + m) * n for m in range(4)]
        out.append(
            {c: (moved[i : i + n, :LANES], moved[i : i + n, LANES:]) for c, i in zip(EVEN, at)}
        )
    return out


def depth_terms(v, inv, pressure, sound, depth, moved):
    lane = lax.broadcasted_iota(jnp.int32, pressure.shape, 1)
    lo, hi, outside = lane == 0, lane == depth - 1, lane >= depth - 1
    q = v[3] * inv
    q_up = jnp.where(hi, -q, up(q, 1))
    p_up = jnp.where(hi, pressure, up(pressure, 1))
    p_dn = jnp.where(lo, pressure, down(pressure, 1))
    wave = jnp.abs(q) + sound
    wave_up = jnp.abs(q_up) + jnp.where(hi, sound, up(sound, 1))
    nu = sensor(p_dn, pressure, p_up)
    k2, k4 = weights(jnp.maximum(nu, jnp.where(hi, nu, up(nu, 1))), wave + wave_up)
    d1 = jnp.where(hi, -v[3], up(v[3], 1)) - v[3]
    d1_dn = jnp.where(lo, v[3] + v[3], down(d1, 1))
    d1_up = jnp.where(hi, d1_dn, up(d1, 1))
    above = {c: x[0] for c, x in moved.items()}
    above[3] = d1 + v[3]
    flux = fluxes(v, q, pressure, 3)
    flux_up = fluxes(above, q_up, p_up, 3)
    out = []
    for c in range(5):
        if c == 3:
            g = (flux[c] + flux_up[c]) - (k2 * d1 - k4 * (d1_up + d1_dn))
            w2, w4 = weights(nu, wave + wave)
            wall = (flux[c] + flux[c]) - (w2 * (v[c] + v[c]) - w4 * (d1 + d1))
            out.append(g - jnp.where(lo, wall, down(g, 1)))
        else:
            g = (flux[c] + flux_up[c]) - (k2 * (above[c] - v[c]) - k4 * moved[c][1])
            g = jnp.where(outside, 0.0, g)
            out.append(g - down(g, 1))
    return out


class Band:
    def __init__(self, base, count):
        self.base, self.count = base, count
        self.tall = -(-count // 8) * 8
        self.cross = -(-(count + 2) // 8) * 8
        self.cols = pl.ds(base, self.tall)


def cross_terms(w, prim, r, band, shift):
    n, base = band.cross, band.base - 1
    vm, v0, v1, v2 = [[w[c, r, pl.ds(base + k, n)] for c in range(5)] for k in (-1, 0, 1, 2)]
    pm, p0, p1 = [prim[1, r, pl.ds(base + k, n)] for k in (-1, 0, 1)]
    q = v0[2] * prim[0, r, pl.ds(base, n)]
    wave = jnp.abs(q) + prim[2, r, pl.ds(base, n)]
    nu = sensor(pm, p0, p1)
    flux = fluxes(v0, q, p0, 2)
    for k, x in enumerate([nu, wave] + flux):
        shift[k, 0:n] = x
    k2, k4 = weights(jnp.maximum(nu, shift[0, 1 : n + 1]), wave + shift[1, 1 : n + 1])
    out = []
    for c in range(5):
        side = (v2[c] - v1[c]) + (v0[c] - vm[c])
        g = (flux[c] + shift[2 + c, 1 : n + 1]) - (k2 * (v1[c] - v0[c]) - k4 * side)
        shift[7 + c, 0:n] = g
        out.append(shift[7 + c, 1 : band.tall + 1] - g[0 : band.tall])
    return out


class Level:
    def __init__(self, depth, fields, carry, shift, matrix):
        self.depth, self.fields, self.carry, self.shift = depth, fields, carry, shift
        self.matrix = matrix
        matrix[...] = depth_matrix(depth)

    def face(self, w, prim, r, band, carry):
        n, cols = band.tall, band.cols
        vm, v0, v1, v2 = [[w[c, r + k, cols] for c in range(5)] for k in (-1, 0, 1, 2)]
        p0, p1, p2 = [prim[1, r + k, cols] for k in (0, 1, 2)]
        q1 = v1[1] * prim[0, r + 1, cols]
        wave1 = jnp.abs(q1) + prim[2, r + 1, cols]
        nu1 = sensor(p0, p1, p2)
        f1 = fluxes(v1, q1, p1, 1)
        nu0 = carry[5, 0:n]
        wave0 = carry[6, 0:n]
        k2, k4 = weights(jnp.maximum(nu0, nu1), wave0 + wave1)
        g = []
        for c in range(5):
            d1 = v1[c] - v0[c]
            side = (v2[c] - v1[c]) + (v0[c] - vm[c])
            g.append((carry[7 + c, 0:n] + f1[c]) - (k2 * d1 - k4 * side))
        carry[5, 0:n] = nu1
        carry[6, 0:n] = wave1
        for c in range(5):
            carry[7 + c, 0:n] = f1[c]
        return g, v0

    def start(self, w, prim, r, band, carry):
        n, cols = band.tall, band.cols
        p = [prim[1, r + k, cols] for k in (-2, -1, 0)]
        v = [w[c, r - 1, cols] for c in range(5)]
        q = v[1] * prim[0, r - 1, cols]
        carry[5, 0:n] = sensor(*p)
        carry[6, 0:n] = jnp.abs(q) + prim[2, r - 1, cols]
        for c, f in enumerate(fluxes(v, q, p[1], 1)):
            carry[7 + c, 0:n] = f
        g, _ = self.face(w, prim, r - 1, band, carry)
        for c in range(5):
            carry[c, 0:n] = g[c]

    def rows(self, w, prim, begins, count, band, sink, unroll=2):
        for k, begin in enumerate(begins):
            self.start(w, prim, begin, band, self.carry.at[k])
        unroll = min(unroll, count)

        @pl.loop(0, count // unroll)
        def _(i):
            jobs = [(k, begin + i * unroll + u) for u in range(unroll) for k, begin in enumerate(begins)]
            vs = [[w[c, r, band.cols] for c in range(5)] for _, r in jobs]
            moved = depth_shifts(vs, self.matrix, self.depth)
            for j, (k, r) in enumerate(jobs):
                carry, shift = self.carry.at[k], self.shift.at[j]
                self.row(w, prim, r, band, sink, carry, shift, moved[j])

    def row(self, w, prim, r, band, sink, carry, shift, moved):
        fields, n, cols = self.fields, band.tall, band.cols
        g, v = self.face(w, prim, r, band, carry)
        total = [g[c] - carry[c, 0:n] for c in range(5)]
        for c in range(5):
            carry[c, 0:n] = g[c]
        part = depth_terms(
            v, prim[0, r, cols], prim[1, r, cols], prim[2, r, cols], self.depth, moved
        )
        total = [a + b for a, b in zip(total, part)]
        part = cross_terms(w, prim, r, band, shift)
        total = [a + b for a, b in zip(total, part)]
        evap = fields[0, r, cols]
        suction = fields[1, r, cols]
        both = suction + fields[2, r, cols]
        total = [
            total[0] + (suction * v[0] - evap),
            total[1] + both * v[1],
            total[2] + both * v[2],
            total[3] + both * v[3],
            total[4] + (suction * v[4] - INFLOW_ENTHALPY * evap),
        ]
        sink(r, v, total, band)


def fill_prim(w, prim, begin, end):
    @pl.loop(begin, end, unroll=4)
    def _(r):
        prim[0, r], prim[1, r], prim[2, r] = primitives([w[c, r] for c in range(5)])


def rate_row(v, pressure, sound, inv):
    wave = (jnp.abs(v[1]) + jnp.abs(v[2]) + jnp.abs(v[3])) * inv + 3.0 * sound
    return (0.5 * CFL_NUMBER) / wave


def store_row(w, prim, r, cols, new):
    for c in range(5):
        w[c, r, cols] = new[c]
    prim[0, r, cols], prim[1, r, cols], prim[2, r, cols] = primitives(new)


def flip8(x):
    sub = lax.broadcasted_iota(jnp.int32, x.shape, 0)
    for step in (1, 2, 4):
        if step == 4:
            x = pltpu.roll(x, 4, 0)
        else:
            x = jnp.where((sub & step) == 0, pltpu.roll(x, 8 - step, 0), pltpu.roll(x, step, 0))
    return x


def mirror(cell, extent):
    return jnp.where(cell < 0, -1 - cell, jnp.where(cell >= extent, 2 * extent - 1 - cell, cell))


def pick(shape, condition):
    a = lax.broadcasted_iota(jnp.int32, shape, 0)
    b = lax.broadcasted_iota(jnp.int32, shape, 1)
    return jnp.where(condition(a, b), 1.0, 0.0)


def matmul(a, b):
    return jnp.dot(a, b, precision=EXACT, preferred_element_type=jnp.float32)


def odd(index, by):
    return (index // by) % 2


def aligned(index):
    return pl.multiple_of(index, 8)


def fine_window(pos, own, ax0, ax1, xs0, xs1, w, ends):
    a, x = odd(pos[0], 1), odd(pos[1], 1)
    for c in range(5):
        w[c, 8:16, 8:24] = own[c]
        w[c, pl.ds(16 * (1 - a), 8), 8:24] = ax0[c]
        w[c, pl.ds(16 * a, 8), 8:24] = ax1[c]
        for slab, at in ((xs0, aligned(24 * (1 - x))), (xs1, aligned(24 * x))):
            w[c, pl.ds(16 - 14 * a, 6), pl.ds(at, 8)] = slab[c, 0:6]
            w[c, 8:16, pl.ds(at, 8)] = slab[c, 6:14]
            w[c, pl.ds(2 + 14 * a, 6), pl.ds(at, 8)] = slab[c, 14:20]

    def cross(at, to, source):
        @pl.when(pos[1] == at)
        def _():
            @pl.loop(2, 22)
            def _(r):
                for c in range(5):
                    x = flip8(w[c, r, source : source + 8])
                    w[c, r, to : to + 8] = -x if c == 2 else x

    cross(0, 0, 8)
    cross(ends[1] - 1, 24, 16)

    def axial(at, to, source, step):
        @pl.when(pos[0] == at)
        def _():
            @pl.loop(0, 8)
            def _(k):
                for c in range(5):
                    x = w[c, source + step * k, 0:32]
                    w[c, to - step * k, 0:32] = -x if c == 1 else x

    axial(0, 7, 8, 1)
    axial(ends[0] - 1, 16, 15, -1)


FINE_PLAN = (
    (((6,), 12, Band(2, 28)), ((2, 18), 4, Band(6, 20))),
    (((6,), 12, Band(4, 24)), ((4, 18), 2, Band(8, 16))),
    (((8,), 8, Band(6, 20)), ((6, 16), 2, Band(8, 16))),
    (((8,), 8, Band(8, 16)),),
)


def fine_relax_kernel(
    ends, pos, own, ax0, ax1, xs0, xs1, fields, out, *rest
):
    slabs, (wa, wb, wc, prim_a, prim_b, rate, carry, shift, matrix) = rest[:-9], rest[-9:]
    fine_window(pos, own, ax0, ax1, xs0, xs1, wa, ends)
    a, x = odd(pos[0], 1), odd(pos[1], 1)
    fill_prim(wa, prim_a, 0, 24)

    @pl.loop(2, 22, unroll=4)
    def _(r):
        rate[r] = rate_row([wa[c, r] for c in range(5)], prim_a[1, r], prim_a[2, r], prim_a[0, r])

    level = Level(LANES, fields, carry, shift, matrix)
    source, source_prim = wa, prim_a
    for k, weight in enumerate(SEGMENT_WEIGHTS):
        last = k == 3
        target = (wb, wc, wb, None)[k]
        target_prim = (prim_b, prim_a, prim_b, None)[k]

        def sink(r, v, total, band, weight=weight, last=last, target=target, prim=target_prim):
            cols = band.cols
            scale = weight * rate[r, cols]
            new = [wa[c, r, cols] - scale * total[c] for c in range(5)]
            if last:
                for c in range(5):
                    out[c, r - 8] = new[c]
                    if slabs:
                        first, final = new[c][0:2], new[c][14:16]
                        slabs[2][c, r - 8] = jnp.where(x == 0, final, first)
                        slabs[3][c, r - 8] = jnp.where(x == 0, first, final)
            else:
                store_row(target, prim, r, cols, new)

        for begins, count, band in FINE_PLAN[k]:
            level.rows(source, source_prim, begins, count, band, sink)
        source, source_prim = target, target_prim
    if slabs:
        for c in range(5):
            for k in range(2):
                slabs[0][c, k] = out[c, 6 * (1 - a) + k]
                slabs[1][c, k] = out[c, 6 * a + k]


def vmem(*shape):
    return pltpu.VMEM(shape, jnp.float32)


def call(kernel, out_shapes, scratch, flops, *args):
    specs = [pl.BlockSpec(memory_space=pltpu.SMEM)]
    specs += [pl.BlockSpec(memory_space=pltpu.VMEM)] * (len(args) - 1)
    single = len(out_shapes) == 1
    outs = [jax.ShapeDtypeStruct(s, jnp.float32) for s in out_shapes]
    out_specs = [pl.BlockSpec(memory_space=pltpu.VMEM)] * len(outs)
    moved = sum(4 * a.size for a in args) + sum(4 * o.size for o in outs)
    return pl.pallas_call(
        kernel,
        out_shape=outs[0] if single else outs,
        in_specs=specs,
        out_specs=out_specs[0] if single else out_specs,
        scratch_shapes=scratch,
        cost_estimate=pl.CostEstimate(flops=flops, bytes_accessed=moved, transcendentals=0),
        interpret=INTERPRET,
    )(*args)


MATRIX = pltpu.VMEM((2 * LANES, 2 * LANES), jnp.bfloat16)
FINE_COLS = 40
MIDDLE_COLS = 32
COARSE_COLS = 24


def fine_relax(ends, pos, own, halos, fields, slabs):
    scratch = [vmem(5, 24, FINE_COLS, LANES)] * 3 + [vmem(3, 24, FINE_COLS, LANES)] * 2
    scratch += [vmem(24, FINE_COLS, LANES), vmem(2, 12, 32, LANES), vmem(4, 12, 40, LANES), MATRIX]
    outs = [own.shape]
    if slabs:
        outs += [(5, 2, 16, LANES)] * 2 + [(5, 8, 2, LANES)] * 2
    return call(
        functools.partial(fine_relax_kernel, ends),
        outs,
        scratch,
        80_000_000,
        pos,
        own,
        *halos,
        fields,
    )


def restrict_rows(ref, scratch, rows, count):
    parts = []
    for c in range(5):
        for r in range(rows // 2):
            scratch[0:count] = ref[c, 2 * r] + ref[c, 2 * r + 1]
            parts.append(
                scratch[pl.ds(0, count // 2, stride=2)] + scratch[pl.ds(1, count // 2, stride=2)]
            )
    return jnp.concatenate(parts, axis=0)


def fine_residual_kernel(
    ends, pos, own, ax0, ax1, xs0, xs1, fields, out, w, prim, res, carry, shift, matrix,
    pair,
):
    a, x = odd(pos[0], 1), odd(pos[1], 1)
    for c in range(5):
        w[c, 2:10, 8:24] = own[c]
        w[c, pl.ds(10 * (1 - a), 2), 8:24] = ax0[c]
        w[c, pl.ds(10 * a, 2), 8:24] = ax1[c]
        w[c, 2:10, 6:8] = jnp.where(x == 1, xs0[c], xs1[c])
        w[c, 2:10, 24:26] = jnp.where(x == 1, xs1[c], xs0[c])

    def cross(at, to, source, step):
        @pl.when(pos[1] == at)
        def _():
            for k in range(2):
                for c in range(5):
                    x = w[c, 2:10, source + step * k : source + step * k + 1]
                    w[c, 2:10, to - step * k : to - step * k + 1] = -x if c == 2 else x

    cross(0, 7, 8, 1)
    cross(ends[1] - 1, 24, 23, -1)

    def axial(at, to, source, step):
        @pl.when(pos[0] == at)
        def _():
            for k in range(2):
                for c in range(5):
                    x = w[c, source + step * k]
                    w[c, to - step * k] = -x if c == 1 else x

    axial(0, 1, 2, 1)
    axial(ends[0] - 1, 10, 9, -1)
    fill_prim(w, prim, 0, 12)

    def sink(r, v, total, band):
        for c in range(5):
            res[c, r - 2] = 0.5 * total[c]

    level = Level(LANES, ShiftedRows(fields, 6), carry, shift, matrix)
    level.rows(w, prim, (2,), 8, Band(8, 16), sink)
    low = pick((LANES, LANES), lambda a, b: a // 2 == b)
    high = pick((LANES, LANES), lambda a, b: a // 2 + 64 == b)
    packed = matmul(0.125 * restrict_rows(own, pair, 8, 16), low)
    packed = packed + matmul(restrict_rows(res, pair, 8, 16), high)
    for c in range(5):
        for r in range(4):
            at = (c * 4 + r) * 8
            out[c, r] = packed[at : at + 8]


class ShiftedRows:
    def __init__(self, ref, by):
        self.ref, self.by = ref, by

    def __getitem__(self, index):
        c, r, cols = index
        return self.ref[c, r + self.by, cols]


def fine_residual(ends, pos, own, halos, fields):
    scratch = [vmem(5, 12, FINE_COLS, LANES), vmem(3, 12, FINE_COLS, LANES)]
    scratch += [vmem(5, 8, 16, LANES), vmem(1, 12, 16, LANES), vmem(2, 12, 32, LANES), MATRIX]
    scratch += [vmem(16, LANES)]
    return call(
        functools.partial(fine_residual_kernel, ends),
        [(5, 4, 8, LANES)],
        scratch,
        8_000_000,
        pos,
        own,
        *halos,
        fields,
    )


def middle_kernel(
    ends, pos, two0, one0, own, one1, two1, xs0, xs1, fields, out, diff,
    v0, wa, wb, force, prim_v, prim_a, prim_b, rate, res, carry, shift, matrix, pair,
):
    a, b, x = odd(pos[0], 1), odd(pos[0], 2), odd(pos[1], 1)
    for c in range(5):
        v0[c, 8:12, 8:16] = own[c]
        for ref, at in (
            (two0, 16 - 16 * b), (one0, 12 - 8 * a), (one1, 4 + 8 * a), (two1, 16 * b)
        ):
            v0[c, pl.ds(at, 4), 8:16] = ref[c]
        for slab, at in ((xs0, aligned(16 * (1 - x))), (xs1, aligned(16 * x))):
            v0[c, pl.ds(16 - 14 * b, 2), pl.ds(at, 8)] = slab[c, 0:2]
            v0[c, pl.ds(12 - 8 * a, 4), pl.ds(at, 8)] = slab[c, 2:6]
            v0[c, 8:12, pl.ds(at, 8)] = slab[c, 6:10]
            v0[c, pl.ds(4 + 8 * a, 4), pl.ds(at, 8)] = slab[c, 10:14]
            v0[c, pl.ds(2 + 14 * b, 2), pl.ds(at, 8)] = slab[c, 14:16]
    begin = 4 * pos[0] - 8
    extent = 4 * ends[0]

    @pl.when((pos[0] < 2) | (pos[0] >= ends[0] - 2))
    def _():
        @pl.loop(0, 20)
        def _(r):
            at = mirror(begin + r, extent) - begin

            @pl.when(at != r)
            def _():
                for c in range(5):
                    x = v0[c, at, 0:24]
                    v0[c, r, 0:24] = -x if c == 1 else x

    def cross(at, to, source):
        @pl.when(pos[1] == at)
        def _():
            @pl.loop(0, 20)
            def _(r):
                for c in range(5):
                    x = flip8(v0[c, r, source : source + 8])
                    v0[c, r, to : to + 8] = -x if c == 2 else x

    cross(0, 0, 8)
    cross(ends[1] - 1, 16, 8)
    level = Level(64, fields, carry, shift, matrix)
    chain(level, MIDDLE_PLAN, 4.0, 20, 24, v0, wa, wb, force, prim_v, prim_a, prim_b, rate, 64)
    inner = pl.ds(8, 8)

    def sink(r, v, total, band):
        for c in range(5):
            res[c, r - 8] = 2.0 * (total[c] + force[c, r, inner])

    level.rows(wb, prim_a, (8,), 4, Band(8, 8), sink, 4)
    valid = lax.broadcasted_iota(jnp.int32, (8, LANES), 1) < 64
    for c in range(5):
        for r in range(4):
            x = wb[c, 8 + r, inner]
            diff[c, r] = jnp.where(valid, x - v0[c, 8 + r, inner], 0.0)
            res[c, r] = jnp.where(valid, res[c, r], 0.0)
            res[5 + c, r] = jnp.where(valid, x, 0.0)
    total = None
    for k, (ref, scale) in enumerate(((res.at[pl.ds(5, 5)], 0.125), (res.at[pl.ds(0, 5)], 1.0))):
        for r in range(2):
            parts = []
            for c in range(5):
                pair[0:8] = ref[c, 2 * r] + ref[c, 2 * r + 1]
                parts.append(
                    pair[pl.ds(0, 4, stride=2)] + pair[pl.ds(1, 4, stride=2)]
                )
                parts.append(jnp.zeros((4, LANES), jnp.float32))
            shift = 64 * r + 32 * k
            m = pick((LANES, LANES), lambda a, b, s=shift: (a // 2 + s == b) & (a < 64))
            part = matmul(scale * jnp.concatenate(parts, axis=0), m)
            total = part if total is None else total + part
    for k in range(out.shape[0]):
        for c in range(5):
            out[k, c] = total[8 * c : 8 * c + 4]


MIDDLE_PLAN = (
    (((6,), 8, Band(2, 20), 2), ((2, 14), 4, Band(6, 12), 1)),
    (((6,), 8, Band(4, 16), 2), ((4, 14), 2, Band(8, 8), 2)),
    (((8,), 4, Band(6, 12), 2), ((6, 12), 2, Band(8, 8), 2)),
)
COARSE_PLAN = (
    (((6,), 2, Band(2, 12), 2), ((2, 8), 4, Band(4, 8), 2)),
    (((4,), 6, Band(4, 8), 3),),
    (((6,), 2, Band(6, 4), 2),),
)


def chain(level, plan, area, rows, cols, v0, wa, wb, force, prim_v, prim_a, prim_b, rate, half):
    @pl.loop(0, rows, unroll=2)
    def _(r):
        every = pl.ds(0, cols)
        v = [v0[c, r, every] for c in range(5)]
        inv, pressure, sound = primitives(v)
        prim_v[0, r, every], prim_v[1, r, every], prim_v[2, r, every] = inv, pressure, sound
        scale = rate_row(v, pressure, sound, inv)
        rate[r, every] = scale
        new = []
        for c in range(5):
            total = (2.0 / area) * pltpu.roll(v[c], LANES - half, 1)
            force[c, r, every] = total
            new.append(v[c] - SEGMENT_WEIGHTS[0] * scale * total)
        store_row(wa, prim_a, r, every, new)

    def force_sink(r, v, total, band):
        for c in range(5):
            force[c, r, band.cols] = force[c, r, band.cols] - total[c]

    for begins, count, band, unroll in plan[0]:
        level.rows(v0, prim_v, begins, count, band, force_sink, unroll)
    source, source_prim = wa, prim_a
    for k in (1, 2, 3):
        target = (wb, wa, wb)[k - 1]
        target_prim = (prim_b, prim_v, prim_a)[k - 1]

        def sink(r, v, total, band, k=k, target=target, prim=target_prim):
            cols = band.cols
            scale = SEGMENT_WEIGHTS[k] * rate[r, cols]
            new = [v0[c, r, cols] - scale * (total[c] + force[c, r, cols]) for c in range(5)]
            store_row(target, prim, r, cols, new)

        for begins, count, band, unroll in plan[k - 1]:
            level.rows(source, source_prim, begins, count, band, sink, unroll)
        source, source_prim = target, target_prim


def middle(ends, pos, pieces, left, right, fields):
    cols = MIDDLE_COLS
    scratch = [vmem(5, 20, cols, LANES)] * 4 + [vmem(3, 20, cols, LANES)] * 3
    scratch += [vmem(20, cols, LANES), vmem(10, 4, 8, LANES), vmem(2, 12, 24, LANES)]
    scratch += [vmem(4, 12, 32, LANES), MATRIX, vmem(8, LANES)]
    return call(
        functools.partial(middle_kernel, ends),
        [(ends[0], 5, 4, LANES), (5, 4, 8, LANES)],
        scratch,
        60_000_000,
        pos,
        *pieces,
        left,
        right,
        fields,
    )


def coarse_kernel(
    ends, pos, own, two0, one0, one1, two1, fields, diff, smoothed, out,
    raw, v0, wa, wb, force, prim_v, prim_a, prim_b, rate, carry, shift, matrix, tall,
    wide,
):
    raw[...] = jnp.zeros_like(raw)
    one, two = odd(pos[1], 1) == 1, odd(pos[1], 2) == 1
    for c in range(5):
        for b in range(7):
            at = pl.ds((c * 7 + b) * LANES, LANES)
            raw[0:4, at] = jnp.where(two, two0[c, b], two1[c, b])
            raw[4:8, at] = jnp.where(one, one0[c, b], one1[c, b])
            raw[8:12, at] = own[c, b]
            raw[12:16, at] = jnp.where(one, one1[c, b], one0[c, b])
            raw[16:20, at] = jnp.where(two, two1[c, b], two0[c, b])
    first = 4 * pos[1] - 6
    extent = 4 * ends[1]
    j = lax.broadcasted_iota(jnp.int32, (16, 24), 0)
    s = lax.broadcasted_iota(jnp.int32, (16, 24), 1)
    cell = mirror(first + j, extent)
    moved = jnp.where(s == cell - first + 2, 1.0, 0.0)
    raw[0:16] = matmul(moved, raw[...])
    row = lax.broadcasted_iota(jnp.int32, (16, LANES), 0) + first
    cross_sign = jnp.where((row < 0) | (row >= extent), -1.0, 1.0)
    begin = 2 * pos[0] - 6
    ax_extent = 2 * ends[0]
    origin = 2 * jnp.clip(pos[0] - 3, 0, ends[0] - 7)

    @pl.loop(0, 14)
    def _(r):
        g = begin + r
        at = mirror(g, ax_extent)
        sign = jnp.where(at == g, 1.0, -1.0)
        block = (at - origin) // 2
        half = (at - origin) % 2
        for c in range(5):
            x = raw[0:16, pl.ds(pl.multiple_of((c * 7 + block) * LANES, LANES), LANES)]
            x = jnp.where(half == 1, pltpu.roll(x, 64, 1), x)
            if c == 1:
                x = x * sign
            if c == 2:
                x = x * cross_sign
            v0[c, r, 0:16] = x

    level = Level(32, fields, carry, shift, matrix)
    chain(level, COARSE_PLAN, 16.0, 14, 16, v0, wa, wb, force, prim_v, prim_a, prim_b, rate, 32)
    lane = lax.broadcasted_iota(jnp.int32, (16, LANES), 1)
    sub = lax.broadcasted_iota(jnp.int32, (16, LANES), 0)
    valid = (lane < 32) & (sub >= 6) & (sub < 10)
    parts = []
    for c in range(5):
        for r in range(2):
            parts.append(jnp.where(valid, wb[c, 6 + r, 0:16] - v0[c, 6 + r, 0:16], 0.0))
    wide[...] = matmul(
        jnp.concatenate(parts, axis=0), pick((LANES, LANES), lambda a, b: a == b // 4)
    )
    parts = [diff[c, r] for c in range(5) for r in range(4)]
    tall[...] = matmul(
        jnp.concatenate(parts, axis=0), pick((LANES, LANES), lambda a, b: a == b // 2)
    )
    four = pick((16, 16), lambda a, b: b == 6 + a // 4)
    two = pick((16, 8), lambda a, b: b == a // 2)
    for c in range(5):
        for r in range(2):
            at = (c * 2 + r) * 16
            big = matmul(four, wide[at : at + 16])
            for m in range(2):
                at = (c * 4 + 2 * r + m) * 8
                step = big + matmul(two, tall[at : at + 8])
                for n in range(2):
                    row = 4 * r + 2 * m + n
                    out[c, row] = smoothed[c, row] + step


def coarse(ends, pos, own, neighbours, fields, diff, smoothed):
    scratch = [vmem(24, 35 * LANES)]
    cols = COARSE_COLS
    scratch += [vmem(5, 14, cols, LANES)] * 4 + [vmem(3, 14, cols, LANES)] * 3
    scratch += [vmem(14, cols, LANES), vmem(2, 12, 16, LANES), vmem(4, 12, 24, LANES), MATRIX]
    scratch += [vmem(160, LANES), vmem(160, LANES)]
    return call(
        functools.partial(coarse_kernel, ends),
        [smoothed.shape],
        scratch,
        20_000_000,
        pos,
        own,
        *neighbours,
        fields,
        diff,
        smoothed,
    )


def swapped(x, axis, by, phase):
    size = lax.axis_size(axis)
    low = [i for i in range(size - by) if (i // by) % 2 == phase]
    pairs = [(i, i + by) for i in low] + [(i + by, i) for i in low]
    return lax.ppermute(x, axis, sorted(pairs))


def wide_halos(own):
    a, x = odd(lax.axis_index("ax"), 1), odd(lax.axis_index("xs"), 1)
    ax1 = swapped(own, "ax", 1, 1)
    ax0 = swapped(own, "ax", 1, 0)

    def slab(phase):
        col = 8 * jnp.where(phase == 0, 1 - x, x)
        parts = [(ax0, 2 * a, 6), (own, 0, 8), (ax1, 2 * (1 - a), 6)]
        return jnp.concatenate(
            [lax.dynamic_slice(y, (0, row, col, 0), (5, n, 8, LANES)) for y, row, n in parts],
            axis=1,
        )

    xs1 = swapped(slab(1), "xs", 1, 1)
    xs0 = swapped(slab(0), "xs", 1, 0)
    return ax0, ax1, xs0, xs1


def wall_terms_kernel(factor, rows, count, origin, ends, pos, code, out, sides):
    extent = 8 * ends[0] // factor
    depth = 16 * ends[1] // factor
    scale = 1.0 / (factor * factor)
    begin = (8 // factor) * pos[0] - origin[0]
    first = (16 // factor) * pos[1] - origin[1]
    lane = lax.broadcasted_iota(jnp.int32, (count, LANES), 1)
    cell = mirror(lax.broadcasted_iota(jnp.int32, (count, LANES), 0) + first, depth)
    kinds = (1, 2, 0)

    def counts(r, kind, side):
        g = mirror(begin + r, extent)
        total = None
        for k in range(factor):
            hit = jnp.where(code[g * factor + k, side : side + 1] == kind, 1.0, 0.0)
            total = hit if total is None else total + hit
        return total

    if factor > 1:

        @pl.loop(0, rows, unroll=2)
        def _(r):
            for t, kind in enumerate(kinds):
                for side in range(2):
                    sides[pl.ds(r * 8 + 2 * t + side, 1)] = counts(r, kind, side)
            sides[pl.ds(r * 8 + 6, 2)] = jnp.zeros((2, LANES), jnp.float32)

        gather = pick((LANES, LANES), lambda a, b: a // factor == b)
        sides[...] = matmul(sides[...], gather)

    inside = cell == lane // factor

    @pl.loop(0, rows, unroll=2)
    def _(r):
        for t, kind in enumerate(kinds):
            edge = []
            for side in range(2):
                if factor > 1:
                    edge.append(sides[pl.ds(r * 8 + 2 * t + side, 1)])
                else:
                    edge.append(counts(r, kind, side))
            for side in (2, 3):
                line = jnp.broadcast_to(counts(r, kind, side), (count, LANES))
                edge.append(jnp.sum(jnp.where(inside, line, 0.0), axis=1, keepdims=True))
            total = jnp.where(cell == 0, edge[0], 0.0) + jnp.where(cell == depth - 1, edge[1], 0.0)
            total = total + jnp.where(lane == 0, edge[2], 0.0)
            total = total + jnp.where(lane == depth - 1, edge[3], 0.0)
            out[t, r] = scale * total


def wall_terms(ends, pos, code, factor, rows, count, origin):
    return call(
        functools.partial(wall_terms_kernel, factor, rows, count, origin, ends),
        [(3, rows, count, LANES)],
        [vmem(rows * 8, LANES)],
        1_000_000,
        pos,
        code,
    )


def per_device(state, wall_code):
    ends = (lax.axis_size("ax"), lax.axis_size("xs"))
    ax, xs = lax.axis_index("ax"), lax.axis_index("xs")
    pos = jnp.stack([ax, xs]).astype(jnp.int32)
    fine_fields = wall_terms(ends, pos, wall_code, 1, 24, FINE_COLS, (8, 8))
    middle_fields = wall_terms(ends, pos, wall_code, 2, 20, MIDDLE_COLS, (8, 8))
    coarse_fields = wall_terms(ends, pos, wall_code, 4, 14, COARSE_COLS, (6, 6))

    smoothed, *slabs = fine_relax(ends, pos, state, wide_halos(state), fine_fields, True)
    halos = [
        swapped(slab, axis, 1, phase)
        for slab, (axis, phase) in zip(slabs, (("ax", 0), ("ax", 1), ("xs", 0), ("xs", 1)))
    ]
    packed = fine_residual(ends, pos, smoothed, halos, fine_fields)

    two0, two1 = [swapped(packed, "ax", 2, phase) for phase in (0, 1)]
    one0, one1 = [swapped(packed, "ax", 1, phase) for phase in (0, 1)]
    b = odd(ax, 2)
    slab = jnp.concatenate(
        [
            lax.dynamic_slice_in_dim(two0, 2 * b, 2, axis=1),
            one0,
            packed,
            one1,
            lax.dynamic_slice_in_dim(two1, 2 * (1 - b), 2, axis=1),
        ],
        axis=1,
    )
    xs0, xs1 = [swapped(slab, "xs", 1, phase) for phase in (0, 1)]
    block, diff = middle(ends, pos, (two0, one0, packed, one1, two1), xs0, xs1, middle_fields)

    column = lax.all_to_all(block, "ax", 0, 0)
    start = jnp.clip(ax - 3, 0, ends[0] - 7)
    column = lax.dynamic_slice_in_dim(column, start, 7, axis=0)
    column = jnp.transpose(column, (1, 0, 2, 3))
    neighbours = [
        swapped(column, "xs", by, phase) for by, phase in ((2, 0), (1, 0), (1, 1), (2, 1))
    ]
    fine_new = coarse(ends, pos, column, neighbours, coarse_fields, diff, smoothed)

    return fine_relax(ends, pos, fine_new, wide_halos(fine_new), fine_fields, False)


def solution(mesh):
    in_specs = (P(None, "ax", "xs", None), P())
    out_specs = P(None, "ax", "xs", None)
    return jax.shard_map(
        per_device, mesh=mesh, in_specs=in_specs, out_specs=out_specs, check_vma=False
    )
```

```python
import functools

import jax
import jax.numpy as jnp
from jax import lax
from jax.experimental import pallas as pl
from jax.experimental.pallas import tpu as pltpu
from jax.sharding import PartitionSpec as P

HEAT_RATIO = 1.4
CFL_NUMBER = 0.8
SECOND_COEF = 0.25
FOURTH_COEF = 0.0625
INFLOW_ENTHALPY = 3.0
SEGMENT_WEIGHTS = (0.25, 1.0 / 3.0, 0.5, 1.0)
LANES = 128
EXACT = lax.Precision.HIGHEST
INTERPRET = False


def up(x, axis):
    return pltpu.roll(x, x.shape[axis] - 1, axis)


def down(x, axis):
    return pltpu.roll(x, 1, axis)


def primitives(v):
    inv = 1.0 / v[0]
    kinetic = 0.5 * (v[1] * v[1] + v[2] * v[2] + v[3] * v[3]) * inv
    pressure = (HEAT_RATIO - 1.0) * (v[4] - kinetic)
    sound = jnp.sqrt(HEAT_RATIO * pressure * inv)
    return inv, pressure, sound


def fluxes(v, q, pressure, d):
    out = [v[d], v[1] * q, v[2] * q, v[3] * q, (v[4] + pressure) * q]
    out[d] = out[d] + pressure
    return out


def sensor(back, here, ahead):
    outer = ahead + back
    twice = here + here
    return jnp.abs(outer - twice) / (outer + twice)


def weights(nu, lam):
    e2 = SECOND_COEF * nu
    e4 = jnp.maximum(FOURTH_COEF - e2, 0.0)
    k4 = lam * e4
    return lam * e2 + (k4 + k4), k4


def depth_matrix(depth):
    a = lax.broadcasted_iota(jnp.int32, (LANES, LANES), 0)
    b = lax.broadcasted_iota(jnp.int32, (LANES, LANES), 1)

    def at(by):
        return jnp.where(a == mirror(b + by, depth), 1.0, 0.0)

    above = at(1)
    half = jnp.concatenate([above, at(2) - above + at(0) - at(-1)], axis=1)
    return jnp.concatenate([half, half], axis=0).astype(jnp.bfloat16)


EVEN = (0, 1, 2, 4)


def depth_shifts(rows, matrix, depth):
    x = jnp.concatenate([v[c] for v in rows for c in EVEN], axis=0)
    if depth < LANES:
        x = jnp.where(lax.broadcasted_iota(jnp.int32, x.shape, 1) < depth, x, 0.0)
    high = x.astype(jnp.bfloat16)
    low = (x - high.astype(jnp.float32)).astype(jnp.bfloat16)
    moved = jnp.dot(
        jnp.concatenate([high, low], axis=1), matrix[...], preferred_element_type=jnp.float32
    )
    n = rows[0][0].shape[0]
    out = []
    for k in range(len(rows)):
        at = [(4 * k + m) * n for m in range(4)]
        out.append(
            {c: (moved[i : i + n, :LANES], moved[i : i + n, LANES:]) for c, i in zip(EVEN, at)}
        )
    return out


def depth_terms(v, inv, pressure, sound, depth, moved):
    lane = lax.broadcasted_iota(jnp.int32, pressure.shape, 1)
    lo, hi, outside = lane == 0, lane == depth - 1, lane >= depth - 1
    q = v[3] * inv
    q_up = jnp.where(hi, -q, up(q, 1))
    p_up = jnp.where(hi, pressure, up(pressure, 1))
    p_dn = jnp.where(lo, pressure, down(pressure, 1))
    wave = jnp.abs(q) + sound
    wave_up = jnp.abs(q_up) + jnp.where(hi, sound, up(sound, 1))
    nu = sensor(p_dn, pressure, p_up)
    k2, k4 = weights(jnp.maximum(nu, jnp.where(hi, nu, up(nu, 1))), wave + wave_up)
    d1 = jnp.where(hi, -v[3], up(v[3], 1)) - v[3]
    d1_dn = jnp.where(lo, v[3] + v[3], down(d1, 1))
    d1_up = jnp.where(hi, d1_dn, up(d1, 1))
    above = {c: x[0] for c, x in moved.items()}
    above[3] = d1 + v[3]
    flux = fluxes(v, q, pressure, 3)
    flux_up = fluxes(above, q_up, p_up, 3)
    out = []
    for c in range(5):
        if c == 3:
            g = (flux[c] + flux_up[c]) - (k2 * d1 - k4 * (d1_up + d1_dn))
            w2, w4 = weights(nu, wave + wave)
            wall = (flux[c] + flux[c]) - (w2 * (v[c] + v[c]) - w4 * (d1 + d1))
            out.append(g - jnp.where(lo, wall, down(g, 1)))
        else:
            g = (flux[c] + flux_up[c]) - (k2 * (above[c] - v[c]) - k4 * moved[c][1])
            g = jnp.where(outside, 0.0, g)
            out.append(g - down(g, 1))
    return out


class Band:
    def __init__(self, base, count):
        self.base, self.count = base, count
        self.tall = -(-count // 8) * 8
        self.cross = -(-(count + 2) // 8) * 8
        self.cols = pl.ds(base, self.tall)


def cross_terms(w, prim, r, band, shift):
    n, base = band.cross, band.base - 1
    vm, v0, v1, v2 = [[w[c, r, pl.ds(base + k, n)] for c in range(5)] for k in (-1, 0, 1, 2)]
    pm, p0, p1 = [prim[1, r, pl.ds(base + k, n)] for k in (-1, 0, 1)]
    q = v0[2] * prim[0, r, pl.ds(base, n)]
    wave = jnp.abs(q) + prim[2, r, pl.ds(base, n)]
    nu = sensor(pm, p0, p1)
    flux = fluxes(v0, q, p0, 2)
    for k, x in enumerate([nu, wave] + flux):
        shift[k, 0:n] = x
    k2, k4 = weights(jnp.maximum(nu, shift[0, 1 : n + 1]), wave + shift[1, 1 : n + 1])
    out = []
    for c in range(5):
        side = (v2[c] - v1[c]) + (v0[c] - vm[c])
        g = (flux[c] + shift[2 + c, 1 : n + 1]) - (k2 * (v1[c] - v0[c]) - k4 * side)
        shift[7 + c, 0:n] = g
        out.append(shift[7 + c, 1 : band.tall + 1] - g[0 : band.tall])
    return out


class Level:
    def __init__(self, depth, fields, carry, shift, matrix):
        self.depth, self.fields, self.carry, self.shift = depth, fields, carry, shift
        self.matrix = matrix
        matrix[...] = depth_matrix(depth)

    def face(self, w, prim, r, band, carry):
        n, cols = band.tall, band.cols
        vm, v0, v1, v2 = [[w[c, r + k, cols] for c in range(5)] for k in (-1, 0, 1, 2)]
        p0, p1, p2 = [prim[1, r + k, cols] for k in (0, 1, 2)]
        q1 = v1[1] * prim[0, r + 1, cols]
        wave1 = jnp.abs(q1) + prim[2, r + 1, cols]
        nu1 = sensor(p0, p1, p2)
        f1 = fluxes(v1, q1, p1, 1)
        nu0 = carry[5, 0:n]
        wave0 = carry[6, 0:n]
        k2, k4 = weights(jnp.maximum(nu0, nu1), wave0 + wave1)
        g = []
        for c in range(5):
            d1 = v1[c] - v0[c]
            side = (v2[c] - v1[c]) + (v0[c] - vm[c])
            g.append((carry[7 + c, 0:n] + f1[c]) - (k2 * d1 - k4 * side))
        carry[5, 0:n] = nu1
        carry[6, 0:n] = wave1
        for c in range(5):
            carry[7 + c, 0:n] = f1[c]
        return g, v0

    def start(self, w, prim, r, band, carry):
        n, cols = band.tall, band.cols
        p = [prim[1, r + k, cols] for k in (-2, -1, 0)]
        v = [w[c, r - 1, cols] for c in range(5)]
        q = v[1] * prim[0, r - 1, cols]
        carry[5, 0:n] = sensor(*p)
        carry[6, 0:n] = jnp.abs(q) + prim[2, r - 1, cols]
        for c, f in enumerate(fluxes(v, q, p[1], 1)):
            carry[7 + c, 0:n] = f
        g, _ = self.face(w, prim, r - 1, band, carry)
        for c in range(5):
            carry[c, 0:n] = g[c]

    def rows(self, w, prim, begins, count, band, sink, unroll=2):
        for k, begin in enumerate(begins):
            self.start(w, prim, begin, band, self.carry.at[k])
        unroll = min(unroll, count)

        @pl.loop(0, count // unroll)
        def _(i):
            jobs = [(k, begin + i * unroll + u) for u in range(unroll) for k, begin in enumerate(begins)]
            vs = [[w[c, r, band.cols] for c in range(5)] for _, r in jobs]
            moved = depth_shifts(vs, self.matrix, self.depth)
            for j, (k, r) in enumerate(jobs):
                carry, shift = self.carry.at[k], self.shift.at[j]
                self.row(w, prim, r, band, sink, carry, shift, moved[j])

    def row(self, w, prim, r, band, sink, carry, shift, moved):
        fields, n, cols = self.fields, band.tall, band.cols
        g, v = self.face(w, prim, r, band, carry)
        total = [g[c] - carry[c, 0:n] for c in range(5)]
        for c in range(5):
            carry[c, 0:n] = g[c]
        part = depth_terms(
            v, prim[0, r, cols], prim[1, r, cols], prim[2, r, cols], self.depth, moved
        )
        total = [a + b for a, b in zip(total, part)]
        part = cross_terms(w, prim, r, band, shift)
        total = [a + b for a, b in zip(total, part)]
        evap = fields[0, r, cols]
        suction = fields[1, r, cols]
        both = suction + fields[2, r, cols]
        total = [
            total[0] + (suction * v[0] - evap),
            total[1] + both * v[1],
            total[2] + both * v[2],
            total[3] + both * v[3],
            total[4] + (suction * v[4] - INFLOW_ENTHALPY * evap),
        ]
        sink(r, v, total, band)


def fill_prim(w, prim, begin, end):
    @pl.loop(begin, end, unroll=4)
    def _(r):
        prim[0, r], prim[1, r], prim[2, r] = primitives([w[c, r] for c in range(5)])


def rate_row(v, pressure, sound, inv):
    wave = (jnp.abs(v[1]) + jnp.abs(v[2]) + jnp.abs(v[3])) * inv + 3.0 * sound
    return (0.5 * CFL_NUMBER) / wave


def store_row(w, prim, r, cols, new):
    for c in range(5):
        w[c, r, cols] = new[c]
    prim[0, r, cols], prim[1, r, cols], prim[2, r, cols] = primitives(new)


def flip8(x):
    sub = lax.broadcasted_iota(jnp.int32, x.shape, 0)
    for step in (1, 2, 4):
        if step == 4:
            x = pltpu.roll(x, 4, 0)
        else:
            x = jnp.where((sub & step) == 0, pltpu.roll(x, 8 - step, 0), pltpu.roll(x, step, 0))
    return x


def mirror(cell, extent):
    return jnp.where(cell < 0, -1 - cell, jnp.where(cell >= extent, 2 * extent - 1 - cell, cell))


def pick(shape, condition):
    a = lax.broadcasted_iota(jnp.int32, shape, 0)
    b = lax.broadcasted_iota(jnp.int32, shape, 1)
    return jnp.where(condition(a, b), 1.0, 0.0)


def matmul(a, b):
    return jnp.dot(a, b, precision=EXACT, preferred_element_type=jnp.float32)


def odd(index, by):
    return (index // by) % 2


def aligned(index):
    return pl.multiple_of(index, 8)


def fine_window(pos, own, ax0, ax1, xs0, xs1, w, ends):
    a, x = odd(pos[0], 1), odd(pos[1], 1)
    for c in range(5):
        w[c, 8:16, 8:24] = own[c]
        w[c, pl.ds(16 * (1 - a), 8), 8:24] = ax0[c]
        w[c, pl.ds(16 * a, 8), 8:24] = ax1[c]
        for slab, at in ((xs0, aligned(24 * (1 - x))), (xs1, aligned(24 * x))):
            w[c, pl.ds(16 - 14 * a, 6), pl.ds(at, 8)] = slab[c, 0:6]
            w[c, 8:16, pl.ds(at, 8)] = slab[c, 6:14]
            w[c, pl.ds(2 + 14 * a, 6), pl.ds(at, 8)] = slab[c, 14:20]

    def cross(at, to, source):
        @pl.when(pos[1] == at)
        def _():
            @pl.loop(2, 22)
            def _(r):
                for c in range(5):
                    x = flip8(w[c, r, source : source + 8])
                    w[c, r, to : to + 8] = -x if c == 2 else x

    cross(0, 0, 8)
    cross(ends[1] - 1, 24, 16)

    def axial(at, to, source, step):
        @pl.when(pos[0] == at)
        def _():
            @pl.loop(0, 8)
            def _(k):
                for c in range(5):
                    x = w[c, source + step * k, 0:32]
                    w[c, to - step * k, 0:32] = -x if c == 1 else x

    axial(0, 7, 8, 1)
    axial(ends[0] - 1, 16, 15, -1)


FINE_PLAN = (
    (((6,), 12, Band(2, 28), 3), ((2, 18), 4, Band(6, 20), 2)),
    (((6,), 12, Band(4, 24), 2), ((4, 18), 2, Band(8, 16), 2)),
    (((8,), 8, Band(6, 20), 4), ((6, 16), 2, Band(8, 16), 2)),
    (((8,), 8, Band(8, 16), 4),),
)


def fine_relax_kernel(
    ends, pos, own, ax0, ax1, xs0, xs1, fields, out, *rest
):
    slabs, (wa, wb, wc, prim_a, prim_b, rate, carry, shift, matrix) = rest[:-9], rest[-9:]
    fine_window(pos, own, ax0, ax1, xs0, xs1, wa, ends)
    a, x = odd(pos[0], 1), odd(pos[1], 1)
    fill_prim(wa, prim_a, 0, 24)

    @pl.loop(2, 22, unroll=4)
    def _(r):
        rate[r] = rate_row([wa[c, r] for c in range(5)], prim_a[1, r], prim_a[2, r], prim_a[0, r])

    level = Level(LANES, fields, carry, shift, matrix)
    source, source_prim = wa, prim_a
    for k, weight in enumerate(SEGMENT_WEIGHTS):
        last = k == 3
        target = (wb, wc, wb, None)[k]
        target_prim = (prim_b, prim_a, prim_b, None)[k]

        def sink(r, v, total, band, weight=weight, last=last, target=target, prim=target_prim):
            cols = band.cols
            scale = weight * rate[r, cols]
            new = [wa[c, r, cols] - scale * total[c] for c in range(5)]
            if last:
                for c in range(5):
                    out[c, r - 8] = new[c]
                    if slabs:
                        first, final = new[c][0:2], new[c][14:16]
                        slabs[2][c, r - 8] = jnp.where(x == 0, final, first)
                        slabs[3][c, r - 8] = jnp.where(x == 0, first, final)
            else:
                store_row(target, prim, r, cols, new)

        for begins, count, band, unroll in FINE_PLAN[k]:
            level.rows(source, source_prim, begins, count, band, sink, unroll)
        source, source_prim = target, target_prim
    if slabs:
        for c in range(5):
            for k in range(2):
                slabs[0][c, k] = out[c, 6 * (1 - a) + k]
                slabs[1][c, k] = out[c, 6 * a + k]


def vmem(*shape):
    return pltpu.VMEM(shape, jnp.float32)


def call(kernel, out_shapes, scratch, flops, *args):
    specs = [pl.BlockSpec(memory_space=pltpu.SMEM)]
    specs += [pl.BlockSpec(memory_space=pltpu.VMEM)] * (len(args) - 1)
    single = len(out_shapes) == 1
    outs = [jax.ShapeDtypeStruct(s, jnp.float32) for s in out_shapes]
    out_specs = [pl.BlockSpec(memory_space=pltpu.VMEM)] * len(outs)
    moved = sum(4 * a.size for a in args) + sum(4 * o.size for o in outs)
    return pl.pallas_call(
        kernel,
        out_shape=outs[0] if single else outs,
        in_specs=specs,
        out_specs=out_specs[0] if single else out_specs,
        scratch_shapes=scratch,
        cost_estimate=pl.CostEstimate(flops=flops, bytes_accessed=moved, transcendentals=0),
        interpret=INTERPRET,
    )(*args)


MATRIX = pltpu.VMEM((2 * LANES, 2 * LANES), jnp.bfloat16)
FINE_COLS = 40
MIDDLE_COLS = 32
COARSE_COLS = 24


def fine_relax(ends, pos, own, halos, fields, slabs):
    scratch = [vmem(5, 24, FINE_COLS, LANES)] * 3 + [vmem(3, 24, FINE_COLS, LANES)] * 2
    scratch += [vmem(24, FINE_COLS, LANES), vmem(2, 12, 32, LANES), vmem(4, 12, 40, LANES), MATRIX]
    outs = [own.shape]
    if slabs:
        outs += [(5, 2, 16, LANES)] * 2 + [(5, 8, 2, LANES)] * 2
    return call(
        functools.partial(fine_relax_kernel, ends),
        outs,
        scratch,
        80_000_000,
        pos,
        own,
        *halos,
        fields,
    )


def restrict_rows(ref, scratch, rows, count):
    parts = []
    for c in range(5):
        for r in range(rows // 2):
            scratch[0:count] = ref[c, 2 * r] + ref[c, 2 * r + 1]
            parts.append(
                scratch[pl.ds(0, count // 2, stride=2)] + scratch[pl.ds(1, count // 2, stride=2)]
            )
    return jnp.concatenate(parts, axis=0)


def fine_residual_kernel(
    ends, pos, own, ax0, ax1, xs0, xs1, fields, out, w, prim, res, carry, shift, matrix,
    pair,
):
    a, x = odd(pos[0], 1), odd(pos[1], 1)
    for c in range(5):
        w[c, 2:10, 8:24] = own[c]
        w[c, pl.ds(10 * (1 - a), 2), 8:24] = ax0[c]
        w[c, pl.ds(10 * a, 2), 8:24] = ax1[c]
        w[c, 2:10, 6:8] = jnp.where(x == 1, xs0[c], xs1[c])
        w[c, 2:10, 24:26] = jnp.where(x == 1, xs1[c], xs0[c])

    def cross(at, to, source, step):
        @pl.when(pos[1] == at)
        def _():
            for k in range(2):
                for c in range(5):
                    x = w[c, 2:10, source + step * k : source + step * k + 1]
                    w[c, 2:10, to - step * k : to - step * k + 1] = -x if c == 2 else x

    cross(0, 7, 8, 1)
    cross(ends[1] - 1, 24, 23, -1)

    def axial(at, to, source, step):
        @pl.when(pos[0] == at)
        def _():
            for k in range(2):
                for c in range(5):
                    x = w[c, source + step * k]
                    w[c, to - step * k] = -x if c == 1 else x

    axial(0, 1, 2, 1)
    axial(ends[0] - 1, 10, 9, -1)
    fill_prim(w, prim, 0, 12)

    def sink(r, v, total, band):
        for c in range(5):
            res[c, r - 2] = 0.5 * total[c]

    level = Level(LANES, ShiftedRows(fields, 6), carry, shift, matrix)
    level.rows(w, prim, (2,), 8, Band(8, 16), sink, 4)
    low = pick((LANES, LANES), lambda a, b: a // 2 == b)
    high = pick((LANES, LANES), lambda a, b: a // 2 + 64 == b)
    packed = matmul(0.125 * restrict_rows(own, pair, 8, 16), low)
    packed = packed + matmul(restrict_rows(res, pair, 8, 16), high)
    for c in range(5):
        for r in range(4):
            at = (c * 4 + r) * 8
            out[c, r] = packed[at : at + 8]


class ShiftedRows:
    def __init__(self, ref, by):
        self.ref, self.by = ref, by

    def __getitem__(self, index):
        c, r, cols = index
        return self.ref[c, r + self.by, cols]


def fine_residual(ends, pos, own, halos, fields):
    scratch = [vmem(5, 12, FINE_COLS, LANES), vmem(3, 12, FINE_COLS, LANES)]
    scratch += [vmem(5, 8, 16, LANES), vmem(1, 12, 16, LANES), vmem(4, 12, 32, LANES), MATRIX]
    scratch += [vmem(16, LANES)]
    return call(
        functools.partial(fine_residual_kernel, ends),
        [(5, 4, 8, LANES)],
        scratch,
        8_000_000,
        pos,
        own,
        *halos,
        fields,
    )


def middle_kernel(
    ends, pos, two0, one0, own, one1, two1, xs0, xs1, fields, out, diff,
    v0, wa, wb, force, prim_v, prim_a, prim_b, rate, res, carry, shift, matrix, pair,
):
    a, b, x = odd(pos[0], 1), odd(pos[0], 2), odd(pos[1], 1)
    for c in range(5):
        v0[c, 8:12, 8:16] = own[c]
        for ref, at in (
            (two0, 16 - 16 * b), (one0, 12 - 8 * a), (one1, 4 + 8 * a), (two1, 16 * b)
        ):
            v0[c, pl.ds(at, 4), 8:16] = ref[c]
        for slab, at in ((xs0, aligned(16 * (1 - x))), (xs1, aligned(16 * x))):
            v0[c, pl.ds(16 - 14 * b, 2), pl.ds(at, 8)] = slab[c, 0:2]
            v0[c, pl.ds(12 - 8 * a, 4), pl.ds(at, 8)] = slab[c, 2:6]
            v0[c, 8:12, pl.ds(at, 8)] = slab[c, 6:10]
            v0[c, pl.ds(4 + 8 * a, 4), pl.ds(at, 8)] = slab[c, 10:14]
            v0[c, pl.ds(2 + 14 * b, 2), pl.ds(at, 8)] = slab[c, 14:16]
    begin = 4 * pos[0] - 8
    extent = 4 * ends[0]

    @pl.when((pos[0] < 2) | (pos[0] >= ends[0] - 2))
    def _():
        @pl.loop(0, 20)
        def _(r):
            at = mirror(begin + r, extent) - begin

            @pl.when(at != r)
            def _():
                for c in range(5):
                    x = v0[c, at, 0:24]
                    v0[c, r, 0:24] = -x if c == 1 else x

    def cross(at, to, source):
        @pl.when(pos[1] == at)
        def _():
            @pl.loop(0, 20)
            def _(r):
                for c in range(5):
                    x = flip8(v0[c, r, source : source + 8])
                    v0[c, r, to : to + 8] = -x if c == 2 else x

    cross(0, 0, 8)
    cross(ends[1] - 1, 16, 8)
    level = Level(64, fields, carry, shift, matrix)
    chain(level, MIDDLE_PLAN, 4.0, 20, 24, v0, wa, wb, force, prim_v, prim_a, prim_b, rate, 64)
    inner = pl.ds(8, 8)

    def sink(r, v, total, band):
        for c in range(5):
            res[c, r - 8] = 2.0 * (total[c] + force[c, r, inner])

    level.rows(wb, prim_a, (8,), 4, Band(8, 8), sink, 4)
    valid = lax.broadcasted_iota(jnp.int32, (8, LANES), 1) < 64
    for c in range(5):
        for r in range(4):
            x = wb[c, 8 + r, inner]
            diff[c, r] = jnp.where(valid, x - v0[c, 8 + r, inner], 0.0)
            res[c, r] = jnp.where(valid, res[c, r], 0.0)
            res[5 + c, r] = jnp.where(valid, x, 0.0)
    total = None
    for k, (ref, scale) in enumerate(((res.at[pl.ds(5, 5)], 0.125), (res.at[pl.ds(0, 5)], 1.0))):
        for r in range(2):
            parts = []
            for c in range(5):
                pair[0:8] = ref[c, 2 * r] + ref[c, 2 * r + 1]
                parts.append(
                    pair[pl.ds(0, 4, stride=2)] + pair[pl.ds(1, 4, stride=2)]
                )
                parts.append(jnp.zeros((4, LANES), jnp.float32))
            shift = 64 * r + 32 * k
            m = pick((LANES, LANES), lambda a, b, s=shift: (a // 2 + s == b) & (a < 64))
            part = matmul(scale * jnp.concatenate(parts, axis=0), m)
            total = part if total is None else total + part
    for k in range(out.shape[0]):
        for c in range(5):
            out[k, c] = total[8 * c : 8 * c + 4]


MIDDLE_PLAN = (
    (((6,), 8, Band(2, 20), 4), ((2, 14), 4, Band(6, 12), 2)),
    (((6,), 8, Band(4, 16), 4), ((4, 14), 2, Band(8, 8), 2)),
    (((8,), 4, Band(6, 12), 4), ((6, 12), 2, Band(8, 8), 2)),
)
COARSE_PLAN = (
    (((6,), 2, Band(2, 12), 2), ((2, 8), 4, Band(4, 8), 4)),
    (((4,), 6, Band(4, 8), 6),),
    (((6,), 2, Band(6, 4), 2),),
)


def chain(level, plan, area, rows, cols, v0, wa, wb, force, prim_v, prim_a, prim_b, rate, half):
    @pl.loop(0, rows, unroll=2)
    def _(r):
        every = pl.ds(0, cols)
        v = [v0[c, r, every] for c in range(5)]
        inv, pressure, sound = primitives(v)
        prim_v[0, r, every], prim_v[1, r, every], prim_v[2, r, every] = inv, pressure, sound
        scale = rate_row(v, pressure, sound, inv)
        rate[r, every] = scale
        new = []
        for c in range(5):
            total = (2.0 / area) * pltpu.roll(v[c], LANES - half, 1)
            force[c, r, every] = total
            new.append(v[c] - SEGMENT_WEIGHTS[0] * scale * total)
        store_row(wa, prim_a, r, every, new)

    def force_sink(r, v, total, band):
        for c in range(5):
            force[c, r, band.cols] = force[c, r, band.cols] - total[c]

    for begins, count, band, unroll in plan[0]:
        level.rows(v0, prim_v, begins, count, band, force_sink, unroll)
    source, source_prim = wa, prim_a
    for k in (1, 2, 3):
        target = (wb, wa, wb)[k - 1]
        target_prim = (prim_b, prim_v, prim_a)[k - 1]

        def sink(r, v, total, band, k=k, target=target, prim=target_prim):
            cols = band.cols
            scale = SEGMENT_WEIGHTS[k] * rate[r, cols]
            new = [v0[c, r, cols] - scale * (total[c] + force[c, r, cols]) for c in range(5)]
            store_row(target, prim, r, cols, new)

        for begins, count, band, unroll in plan[k - 1]:
            level.rows(source, source_prim, begins, count, band, sink, unroll)
        source, source_prim = target, target_prim


def middle(ends, pos, pieces, left, right, fields):
    cols = MIDDLE_COLS
    scratch = [vmem(5, 20, cols, LANES)] * 4 + [vmem(3, 20, cols, LANES)] * 3
    scratch += [vmem(20, cols, LANES), vmem(10, 4, 8, LANES), vmem(2, 12, 24, LANES)]
    scratch += [vmem(4, 12, 32, LANES), MATRIX, vmem(8, LANES)]
    return call(
        functools.partial(middle_kernel, ends),
        [(ends[0], 5, 4, LANES), (5, 4, 8, LANES)],
        scratch,
        60_000_000,
        pos,
        *pieces,
        left,
        right,
        fields,
    )


def coarse_kernel(
    ends, pos, own, two0, one0, one1, two1, fields, diff, smoothed, out,
    raw, v0, wa, wb, force, prim_v, prim_a, prim_b, rate, carry, shift, matrix, tall,
    wide,
):
    raw[...] = jnp.zeros_like(raw)
    one, two = odd(pos[1], 1) == 1, odd(pos[1], 2) == 1
    for c in range(5):
        for b in range(7):
            at = pl.ds((c * 7 + b) * LANES, LANES)
            raw[0:4, at] = jnp.where(two, two0[c, b], two1[c, b])
            raw[4:8, at] = jnp.where(one, one0[c, b], one1[c, b])
            raw[8:12, at] = own[c, b]
            raw[12:16, at] = jnp.where(one, one1[c, b], one0[c, b])
            raw[16:20, at] = jnp.where(two, two1[c, b], two0[c, b])
    first = 4 * pos[1] - 6
    extent = 4 * ends[1]
    j = lax.broadcasted_iota(jnp.int32, (16, 24), 0)
    s = lax.broadcasted_iota(jnp.int32, (16, 24), 1)
    cell = mirror(first + j, extent)
    moved = jnp.where(s == cell - first + 2, 1.0, 0.0)
    raw[0:16] = matmul(moved, raw[...])
    row = lax.broadcasted_iota(jnp.int32, (16, LANES), 0) + first
    cross_sign = jnp.where((row < 0) | (row >= extent), -1.0, 1.0)
    begin = 2 * pos[0] - 6
    ax_extent = 2 * ends[0]
    origin = 2 * jnp.clip(pos[0] - 3, 0, ends[0] - 7)

    @pl.loop(0, 14, unroll=2)
    def _(r):
        g = begin + r
        at = mirror(g, ax_extent)
        sign = jnp.where(at == g, 1.0, -1.0)
        block = (at - origin) // 2
        half = (at - origin) % 2
        for c in range(5):
            x = raw[0:16, pl.ds(pl.multiple_of((c * 7 + block) * LANES, LANES), LANES)]
            x = jnp.where(half == 1, pltpu.roll(x, 64, 1), x)
            if c == 1:
                x = x * sign
            if c == 2:
                x = x * cross_sign
            v0[c, r, 0:16] = x

    level = Level(32, fields, carry, shift, matrix)
    chain(level, COARSE_PLAN, 16.0, 14, 16, v0, wa, wb, force, prim_v, prim_a, prim_b, rate, 32)
    lane = lax.broadcasted_iota(jnp.int32, (16, LANES), 1)
    sub = lax.broadcasted_iota(jnp.int32, (16, LANES), 0)
    valid = (lane < 32) & (sub >= 6) & (sub < 10)
    parts = []
    for c in range(5):
        for r in range(2):
            parts.append(jnp.where(valid, wb[c, 6 + r, 0:16] - v0[c, 6 + r, 0:16], 0.0))
    wide[...] = matmul(
        jnp.concatenate(parts, axis=0), pick((LANES, LANES), lambda a, b: a == b // 4)
    )
    parts = [diff[c, r] for c in range(5) for r in range(4)]
    tall[...] = matmul(
        jnp.concatenate(parts, axis=0), pick((LANES, LANES), lambda a, b: a == b // 2)
    )
    four = pick((16, 16), lambda a, b: b == 6 + a // 4)
    two = pick((16, 8), lambda a, b: b == a // 2)
    for c in range(5):
        for r in range(2):
            at = (c * 2 + r) * 16
            big = matmul(four, wide[at : at + 16])
            for m in range(2):
                at = (c * 4 + 2 * r + m) * 8
                step = big + matmul(two, tall[at : at + 8])
                for n in range(2):
                    row = 4 * r + 2 * m + n
                    out[c, row] = smoothed[c, row] + step


def coarse(ends, pos, own, neighbours, fields, diff, smoothed):
    scratch = [vmem(24, 35 * LANES)]
    cols = COARSE_COLS
    scratch += [vmem(5, 14, cols, LANES)] * 4 + [vmem(3, 14, cols, LANES)] * 3
    scratch += [vmem(14, cols, LANES), vmem(2, 12, 16, LANES), vmem(8, 12, 24, LANES), MATRIX]
    scratch += [vmem(160, LANES), vmem(160, LANES)]
    return call(
        functools.partial(coarse_kernel, ends),
        [smoothed.shape],
        scratch,
        20_000_000,
        pos,
        own,
        *neighbours,
        fields,
        diff,
        smoothed,
    )


def swapped(x, axis, by, phase):
    size = lax.axis_size(axis)
    low = [i for i in range(size - by) if (i // by) % 2 == phase]
    pairs = [(i, i + by) for i in low] + [(i + by, i) for i in low]
    return lax.ppermute(x, axis, sorted(pairs))


def wide_halos(own):
    a, x = odd(lax.axis_index("ax"), 1), odd(lax.axis_index("xs"), 1)
    ax1 = swapped(own, "ax", 1, 1)
    ax0 = swapped(own, "ax", 1, 0)

    def slab(phase):
        col = 8 * jnp.where(phase == 0, 1 - x, x)
        parts = [(ax0, 2 * a, 6), (own, 0, 8), (ax1, 2 * (1 - a), 6)]
        return jnp.concatenate(
            [lax.dynamic_slice(y, (0, row, col, 0), (5, n, 8, LANES)) for y, row, n in parts],
            axis=1,
        )

    xs1 = swapped(slab(1), "xs", 1, 1)
    xs0 = swapped(slab(0), "xs", 1, 0)
    return ax0, ax1, xs0, xs1


def wall_terms_kernel(factor, rows, count, origin, ends, pos, code, out, sides):
    extent = 8 * ends[0] // factor
    depth = 16 * ends[1] // factor
    scale = 1.0 / (factor * factor)
    begin = (8 // factor) * pos[0] - origin[0]
    first = (16 // factor) * pos[1] - origin[1]
    lane = lax.broadcasted_iota(jnp.int32, (count, LANES), 1)
    cell = mirror(lax.broadcasted_iota(jnp.int32, (count, LANES), 0) + first, depth)
    kinds = (1, 2, 0)

    def counts(r, kind, side):
        g = mirror(begin + r, extent)
        total = None
        for k in range(factor):
            hit = jnp.where(code[g * factor + k, side : side + 1] == kind, 1.0, 0.0)
            total = hit if total is None else total + hit
        return total

    if factor > 1:

        @pl.loop(0, rows, unroll=2)
        def _(r):
            for t, kind in enumerate(kinds):
                for side in range(2):
                    sides[pl.ds(r * 8 + 2 * t + side, 1)] = counts(r, kind, side)
            sides[pl.ds(r * 8 + 6, 2)] = jnp.zeros((2, LANES), jnp.float32)

        gather = pick((LANES, LANES), lambda a, b: a // factor == b)
        sides[...] = matmul(sides[...], gather)

    inside = cell == lane // factor

    @pl.loop(0, rows, unroll=2)
    def _(r):
        for t, kind in enumerate(kinds):
            edge = []
            for side in range(2):
                if factor > 1:
                    edge.append(sides[pl.ds(r * 8 + 2 * t + side, 1)])
                else:
                    edge.append(counts(r, kind, side))
            for side in (2, 3):
                line = jnp.broadcast_to(counts(r, kind, side), (count, LANES))
                edge.append(jnp.sum(jnp.where(inside, line, 0.0), axis=1, keepdims=True))
            total = jnp.where(cell == 0, edge[0], 0.0) + jnp.where(cell == depth - 1, edge[1], 0.0)
            total = total + jnp.where(lane == 0, edge[2], 0.0)
            total = total + jnp.where(lane == depth - 1, edge[3], 0.0)
            out[t, r] = scale * total


def wall_terms(ends, pos, code, factor, rows, count, origin):
    return call(
        functools.partial(wall_terms_kernel, factor, rows, count, origin, ends),
        [(3, rows, count, LANES)],
        [vmem(rows * 8, LANES)],
        1_000_000,
        pos,
        code,
    )


def per_device(state, wall_code):
    ends = (lax.axis_size("ax"), lax.axis_size("xs"))
    ax, xs = lax.axis_index("ax"), lax.axis_index("xs")
    pos = jnp.stack([ax, xs]).astype(jnp.int32)
    fine_fields = wall_terms(ends, pos, wall_code, 1, 24, FINE_COLS, (8, 8))
    middle_fields = wall_terms(ends, pos, wall_code, 2, 20, MIDDLE_COLS, (8, 8))
    coarse_fields = wall_terms(ends, pos, wall_code, 4, 14, COARSE_COLS, (6, 6))

    smoothed, *slabs = fine_relax(ends, pos, state, wide_halos(state), fine_fields, True)
    halos = [
        swapped(slab, axis, 1, phase)
        for slab, (axis, phase) in zip(slabs, (("ax", 0), ("ax", 1), ("xs", 0), ("xs", 1)))
    ]
    packed = fine_residual(ends, pos, smoothed, halos, fine_fields)

    two0, two1 = [swapped(packed, "ax", 2, phase) for phase in (0, 1)]
    one0, one1 = [swapped(packed, "ax", 1, phase) for phase in (0, 1)]
    b = odd(ax, 2)
    slab = jnp.concatenate(
        [
            lax.dynamic_slice_in_dim(two0, 2 * b, 2, axis=1),
            one0,
            packed,
            one1,
            lax.dynamic_slice_in_dim(two1, 2 * (1 - b), 2, axis=1),
        ],
        axis=1,
    )
    xs0, xs1 = [swapped(slab, "xs", 1, phase) for phase in (0, 1)]
    block, diff = middle(ends, pos, (two0, one0, packed, one1, two1), xs0, xs1, middle_fields)

    column = lax.all_to_all(block, "ax", 0, 0)
    start = jnp.clip(ax - 3, 0, ends[0] - 7)
    column = lax.dynamic_slice_in_dim(column, start, 7, axis=0)
    column = jnp.transpose(column, (1, 0, 2, 3))
    neighbours = [
        swapped(column, "xs", by, phase) for by, phase in ((2, 0), (1, 0), (1, 1), (2, 1))
    ]
    fine_new = coarse(ends, pos, column, neighbours, coarse_fields, diff, smoothed)

    return fine_relax(ends, pos, fine_new, wide_halos(fine_new), fine_fields, False)


def solution(mesh):
    in_specs = (P(None, "ax", "xs", None), P())
    out_specs = P(None, "ax", "xs", None)
    return jax.shard_map(
        per_device, mesh=mesh, in_specs=in_specs, out_specs=out_specs, check_vma=False
    )
```

```python
import functools

import jax
import jax.numpy as jnp
from jax import lax
from jax.experimental import pallas as pl
from jax.experimental.pallas import tpu as pltpu
from jax.sharding import PartitionSpec as P

HEAT_RATIO = 1.4
CFL_NUMBER = 0.8
SECOND_COEF = 0.25
FOURTH_COEF = 0.0625
INFLOW_ENTHALPY = 3.0
SEGMENT_WEIGHTS = (0.25, 1.0 / 3.0, 0.5, 1.0)
LANES = 128
EXACT = lax.Precision.HIGHEST
INTERPRET = False


def up(x, axis):
    return pltpu.roll(x, x.shape[axis] - 1, axis)


def down(x, axis):
    return pltpu.roll(x, 1, axis)


def primitives(v):
    inv = 1.0 / v[0]
    kinetic = 0.5 * (v[1] * v[1] + v[2] * v[2] + v[3] * v[3]) * inv
    pressure = (HEAT_RATIO - 1.0) * (v[4] - kinetic)
    sound = jnp.sqrt(HEAT_RATIO * pressure * inv)
    return inv, pressure, sound


def fluxes(v, q, pressure, d):
    out = [v[d], v[1] * q, v[2] * q, v[3] * q, (v[4] + pressure) * q]
    out[d] = out[d] + pressure
    return out


def sensor(back, here, ahead):
    outer = ahead + back
    twice = here + here
    return jnp.abs(outer - twice) / (outer + twice)


def weights(nu, lam):
    e2 = SECOND_COEF * nu
    e4 = jnp.maximum(FOURTH_COEF - e2, 0.0)
    k4 = lam * e4
    return lam * e2 + (k4 + k4), k4


def depth_matrix(depth):
    a = lax.broadcasted_iota(jnp.int32, (LANES, LANES), 0)
    b = lax.broadcasted_iota(jnp.int32, (LANES, LANES), 1)

    def at(by):
        return jnp.where(a == mirror(b + by, depth), 1.0, 0.0)

    above = at(1)
    half = jnp.concatenate([above, at(2) - above + at(0) - at(-1)], axis=1)
    return jnp.concatenate([half, half], axis=0).astype(jnp.bfloat16)


EVEN = (0, 1, 2, 4)


def depth_shifts(rows, matrix, depth):
    x = jnp.concatenate([v[c] for v in rows for c in EVEN], axis=0)
    if depth < LANES:
        x = jnp.where(lax.broadcasted_iota(jnp.int32, x.shape, 1) < depth, x, 0.0)
    high = x.astype(jnp.bfloat16)
    low = (x - high.astype(jnp.float32)).astype(jnp.bfloat16)
    moved = jnp.dot(
        jnp.concatenate([high, low], axis=1), matrix[...], preferred_element_type=jnp.float32
    )
    n = rows[0][0].shape[0]
    out = []
    for k in range(len(rows)):
        at = [(4 * k + m) * n for m in range(4)]
        out.append(
            {c: (moved[i : i + n, :LANES], moved[i : i + n, LANES:]) for c, i in zip(EVEN, at)}
        )
    return out


def depth_terms(v, inv, pressure, sound, depth, moved):
    lane = lax.broadcasted_iota(jnp.int32, pressure.shape, 1)
    lo, hi, outside = lane == 0, lane == depth - 1, lane >= depth - 1
    q = v[3] * inv
    q_up = jnp.where(hi, -q, up(q, 1))
    p_up = jnp.where(hi, pressure, up(pressure, 1))
    p_dn = jnp.where(lo, pressure, down(pressure, 1))
    wave = jnp.abs(q) + sound
    wave_up = jnp.abs(q_up) + jnp.where(hi, sound, up(sound, 1))
    nu = sensor(p_dn, pressure, p_up)
    k2, k4 = weights(jnp.maximum(nu, jnp.where(hi, nu, up(nu, 1))), wave + wave_up)
    d1 = jnp.where(hi, -v[3], up(v[3], 1)) - v[3]
    d1_dn = jnp.where(lo, v[3] + v[3], down(d1, 1))
    d1_up = jnp.where(hi, d1_dn, up(d1, 1))
    above = {c: x[0] for c, x in moved.items()}
    above[3] = d1 + v[3]
    flux = fluxes(v, q, pressure, 3)
    flux_up = fluxes(above, q_up, p_up, 3)
    out = []
    for c in range(5):
        if c == 3:
            g = (flux[c] + flux_up[c]) - (k2 * d1 - k4 * (d1_up + d1_dn))
            w2, w4 = weights(nu, wave + wave)
            wall = (flux[c] + flux[c]) - (w2 * (v[c] + v[c]) - w4 * (d1 + d1))
            out.append(g - jnp.where(lo, wall, down(g, 1)))
        else:
            g = (flux[c] + flux_up[c]) - (k2 * (above[c] - v[c]) - k4 * moved[c][1])
            g = jnp.where(outside, 0.0, g)
            out.append(g - down(g, 1))
    return out


class Band:
    def __init__(self, base, count):
        self.base, self.count = base, count
        self.tall = -(-count // 8) * 8
        self.cross = -(-(count + 2) // 8) * 8
        self.cols = pl.ds(base, self.tall)


def cross_terms(w, prim, r, band, shift):
    n, base = band.cross, band.base - 1
    vm, v0, v1, v2 = [[w[c, r, pl.ds(base + k, n)] for c in range(5)] for k in (-1, 0, 1, 2)]
    pm, p0, p1 = [prim[1, r, pl.ds(base + k, n)] for k in (-1, 0, 1)]
    q = v0[2] * prim[0, r, pl.ds(base, n)]
    wave = jnp.abs(q) + prim[2, r, pl.ds(base, n)]
    nu = sensor(pm, p0, p1)
    flux = fluxes(v0, q, p0, 2)
    for k, x in enumerate([nu, wave] + flux):
        shift[k, 0:n] = x
    k2, k4 = weights(jnp.maximum(nu, shift[0, 1 : n + 1]), wave + shift[1, 1 : n + 1])
    out = []
    for c in range(5):
        side = (v2[c] - v1[c]) + (v0[c] - vm[c])
        g = (flux[c] + shift[2 + c, 1 : n + 1]) - (k2 * (v1[c] - v0[c]) - k4 * side)
        shift[7 + c, 0:n] = g
        out.append(shift[7 + c, 1 : band.tall + 1] - g[0 : band.tall])
    return out


class Level:
    def __init__(self, depth, fields, carry, shift, matrix):
        self.depth, self.fields, self.carry, self.shift = depth, fields, carry, shift
        self.matrix = matrix
        matrix[...] = depth_matrix(depth)

    def face(self, w, prim, r, band, carry):
        n, cols = band.tall, band.cols
        vm, v0, v1, v2 = [[w[c, r + k, cols] for c in range(5)] for k in (-1, 0, 1, 2)]
        p0, p1, p2 = [prim[1, r + k, cols] for k in (0, 1, 2)]
        q1 = v1[1] * prim[0, r + 1, cols]
        wave1 = jnp.abs(q1) + prim[2, r + 1, cols]
        nu1 = sensor(p0, p1, p2)
        f1 = fluxes(v1, q1, p1, 1)
        nu0 = carry[5, 0:n]
        wave0 = carry[6, 0:n]
        k2, k4 = weights(jnp.maximum(nu0, nu1), wave0 + wave1)
        g = []
        for c in range(5):
            d1 = v1[c] - v0[c]
            side = (v2[c] - v1[c]) + (v0[c] - vm[c])
            g.append((carry[7 + c, 0:n] + f1[c]) - (k2 * d1 - k4 * side))
        carry[5, 0:n] = nu1
        carry[6, 0:n] = wave1
        for c in range(5):
            carry[7 + c, 0:n] = f1[c]
        return g, v0

    def start(self, w, prim, r, band, carry):
        n, cols = band.tall, band.cols
        p = [prim[1, r + k, cols] for k in (-2, -1, 0)]
        v = [w[c, r - 1, cols] for c in range(5)]
        q = v[1] * prim[0, r - 1, cols]
        carry[5, 0:n] = sensor(*p)
        carry[6, 0:n] = jnp.abs(q) + prim[2, r - 1, cols]
        for c, f in enumerate(fluxes(v, q, p[1], 1)):
            carry[7 + c, 0:n] = f
        g, _ = self.face(w, prim, r - 1, band, carry)
        for c in range(5):
            carry[c, 0:n] = g[c]

    def rows(self, w, prim, begins, count, band, sink, unroll=2):
        for k, begin in enumerate(begins):
            self.start(w, prim, begin, band, self.carry.at[k])
        unroll = min(unroll, count)

        @pl.loop(0, count // unroll)
        def _(i):
            jobs = [(k, begin + i * unroll + u) for u in range(unroll) for k, begin in enumerate(begins)]
            vs = [[w[c, r, band.cols] for c in range(5)] for _, r in jobs]
            moved = depth_shifts(vs, self.matrix, self.depth)
            for j, (k, r) in enumerate(jobs):
                carry, shift = self.carry.at[k], self.shift.at[j]
                self.row(w, prim, r, band, sink, carry, shift, moved[j])

    def row(self, w, prim, r, band, sink, carry, shift, moved):
        fields, n, cols = self.fields, band.tall, band.cols
        g, v = self.face(w, prim, r, band, carry)
        total = [g[c] - carry[c, 0:n] for c in range(5)]
        for c in range(5):
            carry[c, 0:n] = g[c]
        part = depth_terms(
            v, prim[0, r, cols], prim[1, r, cols], prim[2, r, cols], self.depth, moved
        )
        total = [a + b for a, b in zip(total, part)]
        part = cross_terms(w, prim, r, band, shift)
        total = [a + b for a, b in zip(total, part)]
        evap = fields[0, r, cols]
        suction = fields[1, r, cols]
        both = suction + fields[2, r, cols]
        total = [
            total[0] + (suction * v[0] - evap),
            total[1] + both * v[1],
            total[2] + both * v[2],
            total[3] + both * v[3],
            total[4] + (suction * v[4] - INFLOW_ENTHALPY * evap),
        ]
        sink(r, v, total, band)


def fill_prim(w, prim, begin, end):
    @pl.loop(begin, end, unroll=4)
    def _(r):
        prim[0, r], prim[1, r], prim[2, r] = primitives([w[c, r] for c in range(5)])


def rate_row(v, pressure, sound, inv):
    wave = (jnp.abs(v[1]) + jnp.abs(v[2]) + jnp.abs(v[3])) * inv + 3.0 * sound
    return (0.5 * CFL_NUMBER) / wave


def store_row(w, prim, r, cols, new):
    for c in range(5):
        w[c, r, cols] = new[c]
    prim[0, r, cols], prim[1, r, cols], prim[2, r, cols] = primitives(new)


def flip8(x):
    sub = lax.broadcasted_iota(jnp.int32, x.shape, 0)
    for step in (1, 2, 4):
        if step == 4:
            x = pltpu.roll(x, 4, 0)
        else:
            x = jnp.where((sub & step) == 0, pltpu.roll(x, 8 - step, 0), pltpu.roll(x, step, 0))
    return x


def mirror(cell, extent):
    return jnp.where(cell < 0, -1 - cell, jnp.where(cell >= extent, 2 * extent - 1 - cell, cell))


def pick(shape, condition):
    a = lax.broadcasted_iota(jnp.int32, shape, 0)
    b = lax.broadcasted_iota(jnp.int32, shape, 1)
    return jnp.where(condition(a, b), 1.0, 0.0)


def matmul(a, b):
    return jnp.dot(a, b, precision=EXACT, preferred_element_type=jnp.float32)


def odd(index, by):
    return (index // by) % 2


def aligned(index):
    return pl.multiple_of(index, 8)


def fine_window(pos, own, ax0, ax1, xs0, xs1, w, ends):
    a, x = odd(pos[0], 1), odd(pos[1], 1)
    for c in range(5):
        w[c, 8:16, 8:24] = own[c]
        w[c, pl.ds(16 * (1 - a), 8), 8:24] = ax0[c]
        w[c, pl.ds(16 * a, 8), 8:24] = ax1[c]
        for slab, at in ((xs0, aligned(24 * (1 - x))), (xs1, aligned(24 * x))):
            w[c, pl.ds(16 - 14 * a, 6), pl.ds(at, 8)] = slab[c, 0:6]
            w[c, 8:16, pl.ds(at, 8)] = slab[c, 6:14]
            w[c, pl.ds(2 + 14 * a, 6), pl.ds(at, 8)] = slab[c, 14:20]

    def cross(at, to, source):
        @pl.when(pos[1] == at)
        def _():
            @pl.loop(2, 22)
            def _(r):
                for c in range(5):
                    x = flip8(w[c, r, source : source + 8])
                    w[c, r, to : to + 8] = -x if c == 2 else x

    cross(0, 0, 8)
    cross(ends[1] - 1, 24, 16)

    def axial(at, to, source, step):
        @pl.when(pos[0] == at)
        def _():
            @pl.loop(0, 8)
            def _(k):
                for c in range(5):
                    x = w[c, source + step * k, 0:32]
                    w[c, to - step * k, 0:32] = -x if c == 1 else x

    axial(0, 7, 8, 1)
    axial(ends[0] - 1, 16, 15, -1)


FINE_PLAN = (
    (((6,), 12, Band(2, 28), 3), ((2, 18), 4, Band(6, 20), 2)),
    (((6,), 12, Band(4, 24), 2), ((4, 18), 2, Band(8, 16), 2)),
    (((8,), 8, Band(6, 20), 4), ((6, 16), 2, Band(8, 16), 2)),
    (((8,), 8, Band(8, 16), 4),),
)


def fine_relax_kernel(
    ends, pos, own, ax0, ax1, xs0, xs1, fields, out, *rest
):
    slabs, (wa, wb, wc, prim_a, prim_b, rate, carry, shift, matrix) = rest[:-9], rest[-9:]
    fine_window(pos, own, ax0, ax1, xs0, xs1, wa, ends)
    a, x = odd(pos[0], 1), odd(pos[1], 1)
    fill_prim(wa, prim_a, 0, 24)

    @pl.loop(2, 22, unroll=4)
    def _(r):
        rate[r] = rate_row([wa[c, r] for c in range(5)], prim_a[1, r], prim_a[2, r], prim_a[0, r])

    level = Level(LANES, fields, carry, shift, matrix)
    source, source_prim = wa, prim_a
    for k, weight in enumerate(SEGMENT_WEIGHTS):
        last = k == 3
        target = (wb, wc, wb, None)[k]
        target_prim = (prim_b, prim_a, prim_b, None)[k]

        def sink(r, v, total, band, weight=weight, last=last, target=target, prim=target_prim):
            cols = band.cols
            scale = weight * rate[r, cols]
            new = [wa[c, r, cols] - scale * total[c] for c in range(5)]
            if last:
                for c in range(5):
                    out[c, r - 8] = new[c]
                    if slabs:
                        first, final = new[c][0:2], new[c][14:16]
                        slabs[2][c, r - 8] = jnp.where(x == 0, final, first)
                        slabs[3][c, r - 8] = jnp.where(x == 0, first, final)
            else:
                store_row(target, prim, r, cols, new)

        for begins, count, band, unroll in FINE_PLAN[k]:
            level.rows(source, source_prim, begins, count, band, sink, unroll)
        source, source_prim = target, target_prim
    if slabs:
        for c in range(5):
            for k in range(2):
                slabs[0][c, k] = out[c, 6 * (1 - a) + k]
                slabs[1][c, k] = out[c, 6 * a + k]


def vmem(*shape):
    return pltpu.VMEM(shape, jnp.float32)


def call(kernel, out_shapes, scratch, flops, *args):
    specs = [pl.BlockSpec(memory_space=pltpu.SMEM)]
    specs += [pl.BlockSpec(memory_space=pltpu.VMEM)] * (len(args) - 1)
    single = len(out_shapes) == 1
    outs = [jax.ShapeDtypeStruct(s, jnp.float32) for s in out_shapes]
    out_specs = [pl.BlockSpec(memory_space=pltpu.VMEM)] * len(outs)
    moved = sum(4 * a.size for a in args) + sum(4 * o.size for o in outs)
    return pl.pallas_call(
        kernel,
        out_shape=outs[0] if single else outs,
        in_specs=specs,
        out_specs=out_specs[0] if single else out_specs,
        scratch_shapes=scratch,
        cost_estimate=pl.CostEstimate(flops=flops, bytes_accessed=moved, transcendentals=0),
        interpret=INTERPRET,
    )(*args)


MATRIX = pltpu.VMEM((2 * LANES, 2 * LANES), jnp.bfloat16)
FINE_COLS = 40
MIDDLE_COLS = 32
COARSE_COLS = 24


def fine_relax(ends, pos, own, halos, fields, slabs):
    scratch = [vmem(5, 24, FINE_COLS, LANES)] * 3 + [vmem(3, 24, FINE_COLS, LANES)] * 2
    scratch += [vmem(24, FINE_COLS, LANES), vmem(2, 12, 32, LANES), vmem(4, 12, 40, LANES), MATRIX]
    outs = [own.shape]
    if slabs:
        outs += [(5, 2, 16, LANES)] * 2 + [(5, 8, 2, LANES)] * 2
    return call(
        functools.partial(fine_relax_kernel, ends),
        outs,
        scratch,
        80_000_000,
        pos,
        own,
        *halos,
        fields,
    )


def restrict_rows(ref, scratch, rows, count):
    parts = []
    for c in range(5):
        for r in range(rows // 2):
            scratch[0:count] = ref[c, 2 * r] + ref[c, 2 * r + 1]
            parts.append(
                scratch[pl.ds(0, count // 2, stride=2)] + scratch[pl.ds(1, count // 2, stride=2)]
            )
    return jnp.concatenate(parts, axis=0)


def fine_residual_kernel(
    ends, pos, own, ax0, ax1, xs0, xs1, fields, out, w, prim, res, carry, shift, matrix,
    pair,
):
    a, x = odd(pos[0], 1), odd(pos[1], 1)
    for c in range(5):
        w[c, 2:10, 8:24] = own[c]
        w[c, pl.ds(10 * (1 - a), 2), 8:24] = ax0[c]
        w[c, pl.ds(10 * a, 2), 8:24] = ax1[c]
        w[c, 2:10, 6:8] = jnp.where(x == 1, xs0[c], xs1[c])
        w[c, 2:10, 24:26] = jnp.where(x == 1, xs1[c], xs0[c])

    def cross(at, to, source, step):
        @pl.when(pos[1] == at)
        def _():
            for k in range(2):
                for c in range(5):
                    x = w[c, 2:10, source + step * k : source + step * k + 1]
                    w[c, 2:10, to - step * k : to - step * k + 1] = -x if c == 2 else x

    cross(0, 7, 8, 1)
    cross(ends[1] - 1, 24, 23, -1)

    def axial(at, to, source, step):
        @pl.when(pos[0] == at)
        def _():
            for k in range(2):
                for c in range(5):
                    x = w[c, source + step * k]
                    w[c, to - step * k] = -x if c == 1 else x

    axial(0, 1, 2, 1)
    axial(ends[0] - 1, 10, 9, -1)
    fill_prim(w, prim, 0, 12)

    def sink(r, v, total, band):
        for c in range(5):
            res[c, r - 2] = 0.5 * total[c]

    level = Level(LANES, ShiftedRows(fields, 6), carry, shift, matrix)
    level.rows(w, prim, (2,), 8, Band(8, 16), sink, 4)
    low = pick((LANES, LANES), lambda a, b: a // 2 == b)
    high = pick((LANES, LANES), lambda a, b: a // 2 + 64 == b)
    packed = matmul(0.125 * restrict_rows(own, pair, 8, 16), low)
    packed = packed + matmul(restrict_rows(res, pair, 8, 16), high)
    for c in range(5):
        for r in range(4):
            at = (c * 4 + r) * 8
            out[c, r] = packed[at : at + 8]


class ShiftedRows:
    def __init__(self, ref, by):
        self.ref, self.by = ref, by

    def __getitem__(self, index):
        c, r, cols = index
        return self.ref[c, r + self.by, cols]


def fine_residual(ends, pos, own, halos, fields):
    scratch = [vmem(5, 12, FINE_COLS, LANES), vmem(3, 12, FINE_COLS, LANES)]
    scratch += [vmem(5, 8, 16, LANES), vmem(1, 12, 16, LANES), vmem(4, 12, 32, LANES), MATRIX]
    scratch += [vmem(16, LANES)]
    return call(
        functools.partial(fine_residual_kernel, ends),
        [(5, 4, 8, LANES)],
        scratch,
        8_000_000,
        pos,
        own,
        *halos,
        fields,
    )


def middle_kernel(
    ends, pos, two0, one0, own, one1, two1, xs0, xs1, fields, out, diff,
    v0, wa, wb, force, prim_v, prim_a, prim_b, rate, res, carry, shift, matrix, pair,
):
    a, b, x = odd(pos[0], 1), odd(pos[0], 2), odd(pos[1], 1)
    for c in range(5):
        v0[c, 8:12, 8:16] = own[c]
        for ref, at in (
            (two0, 16 - 16 * b), (one0, 12 - 8 * a), (one1, 4 + 8 * a), (two1, 16 * b)
        ):
            v0[c, pl.ds(at, 4), 8:16] = ref[c]
        for slab, at in ((xs0, aligned(16 * (1 - x))), (xs1, aligned(16 * x))):
            v0[c, pl.ds(16 - 14 * b, 2), pl.ds(at, 8)] = slab[c, 0:2]
            v0[c, pl.ds(12 - 8 * a, 4), pl.ds(at, 8)] = slab[c, 2:6]
            v0[c, 8:12, pl.ds(at, 8)] = slab[c, 6:10]
            v0[c, pl.ds(4 + 8 * a, 4), pl.ds(at, 8)] = slab[c, 10:14]
            v0[c, pl.ds(2 + 14 * b, 2), pl.ds(at, 8)] = slab[c, 14:16]
    begin = 4 * pos[0] - 8
    extent = 4 * ends[0]

    @pl.when((pos[0] < 2) | (pos[0] >= ends[0] - 2))
    def _():
        @pl.loop(0, 20)
        def _(r):
            at = mirror(begin + r, extent) - begin

            @pl.when(at != r)
            def _():
                for c in range(5):
                    x = v0[c, at, 0:24]
                    v0[c, r, 0:24] = -x if c == 1 else x

    def cross(at, to, source):
        @pl.when(pos[1] == at)
        def _():
            @pl.loop(0, 20)
            def _(r):
                for c in range(5):
                    x = flip8(v0[c, r, source : source + 8])
                    v0[c, r, to : to + 8] = -x if c == 2 else x

    cross(0, 0, 8)
    cross(ends[1] - 1, 16, 8)
    level = Level(64, fields, carry, shift, matrix)
    chain(level, MIDDLE_PLAN, 4.0, 20, 24, v0, wa, wb, force, prim_v, prim_a, prim_b, rate, 64)
    inner = pl.ds(8, 8)

    def sink(r, v, total, band):
        for c in range(5):
            res[c, r - 8] = 2.0 * (total[c] + force[c, r, inner])

    level.rows(wb, prim_a, (8,), 4, Band(8, 8), sink, 4)
    valid = lax.broadcasted_iota(jnp.int32, (8, LANES), 1) < 64
    for c in range(5):
        for r in range(4):
            x = wb[c, 8 + r, inner]
            diff[c, r] = jnp.where(valid, x - v0[c, 8 + r, inner], 0.0)
            res[c, r] = jnp.where(valid, res[c, r], 0.0)
            res[5 + c, r] = jnp.where(valid, x, 0.0)
    total = None
    for k, (ref, scale) in enumerate(((res.at[pl.ds(5, 5)], 0.125), (res.at[pl.ds(0, 5)], 1.0))):
        for r in range(2):
            parts = []
            for c in range(5):
                pair[0:8] = ref[c, 2 * r] + ref[c, 2 * r + 1]
                parts.append(
                    pair[pl.ds(0, 4, stride=2)] + pair[pl.ds(1, 4, stride=2)]
                )
                parts.append(jnp.zeros((4, LANES), jnp.float32))
            shift = 64 * r + 32 * k
            m = pick((LANES, LANES), lambda a, b, s=shift: (a // 2 + s == b) & (a < 64))
            part = matmul(scale * jnp.concatenate(parts, axis=0), m)
            total = part if total is None else total + part
    for k in range(out.shape[0]):
        for c in range(5):
            out[k, c] = total[8 * c : 8 * c + 4]


MIDDLE_PLAN = (
    (((6,), 8, Band(2, 20), 4), ((2, 14), 4, Band(6, 12), 2)),
    (((6,), 8, Band(4, 16), 4), ((4, 14), 2, Band(8, 8), 2)),
    (((8,), 4, Band(6, 12), 4), ((6, 12), 2, Band(8, 8), 2)),
)
COARSE_PLAN = (
    (((6,), 2, Band(2, 12), 2), ((2, 8), 4, Band(4, 8), 4)),
    (((4,), 6, Band(4, 8), 6),),
    (((6,), 2, Band(6, 4), 2),),
)


def chain(level, plan, area, rows, cols, v0, wa, wb, force, prim_v, prim_a, prim_b, rate, half):
    @pl.loop(0, rows, unroll=4 if rows % 4 == 0 else 7)
    def _(r):
        every = pl.ds(0, cols)
        v = [v0[c, r, every] for c in range(5)]
        inv, pressure, sound = primitives(v)
        prim_v[0, r, every], prim_v[1, r, every], prim_v[2, r, every] = inv, pressure, sound
        scale = rate_row(v, pressure, sound, inv)
        rate[r, every] = scale
        new = []
        for c in range(5):
            total = (2.0 / area) * pltpu.roll(v[c], LANES - half, 1)
            force[c, r, every] = total
            new.append(v[c] - SEGMENT_WEIGHTS[0] * scale * total)
        store_row(wa, prim_a, r, every, new)

    def force_sink(r, v, total, band):
        for c in range(5):
            force[c, r, band.cols] = force[c, r, band.cols] - total[c]

    for begins, count, band, unroll in plan[0]:
        level.rows(v0, prim_v, begins, count, band, force_sink, unroll)
    source, source_prim = wa, prim_a
    for k in (1, 2, 3):
        target = (wb, wa, wb)[k - 1]
        target_prim = (prim_b, prim_v, prim_a)[k - 1]

        def sink(r, v, total, band, k=k, target=target, prim=target_prim):
            cols = band.cols
            scale = SEGMENT_WEIGHTS[k] * rate[r, cols]
            new = [v0[c, r, cols] - scale * (total[c] + force[c, r, cols]) for c in range(5)]
            store_row(target, prim, r, cols, new)

        for begins, count, band, unroll in plan[k - 1]:
            level.rows(source, source_prim, begins, count, band, sink, unroll)
        source, source_prim = target, target_prim


def middle(ends, pos, pieces, left, right, fields):
    cols = MIDDLE_COLS
    scratch = [vmem(5, 20, cols, LANES)] * 4 + [vmem(3, 20, cols, LANES)] * 3
    scratch += [vmem(20, cols, LANES), vmem(10, 4, 8, LANES), vmem(2, 12, 24, LANES)]
    scratch += [vmem(4, 12, 32, LANES), MATRIX, vmem(8, LANES)]
    return call(
        functools.partial(middle_kernel, ends),
        [(ends[0], 5, 4, LANES), (5, 4, 8, LANES)],
        scratch,
        60_000_000,
        pos,
        *pieces,
        left,
        right,
        fields,
    )


def coarse_kernel(
    ends, pos, own, two0, one0, one1, two1, fields, diff, smoothed, out,
    raw, v0, wa, wb, force, prim_v, prim_a, prim_b, rate, carry, shift, matrix, tall,
    wide,
):
    raw[...] = jnp.zeros_like(raw)
    one, two = odd(pos[1], 1) == 1, odd(pos[1], 2) == 1
    for c in range(5):
        for b in range(7):
            at = pl.ds((c * 7 + b) * LANES, LANES)
            raw[0:4, at] = jnp.where(two, two0[c, b], two1[c, b])
            raw[4:8, at] = jnp.where(one, one0[c, b], one1[c, b])
            raw[8:12, at] = own[c, b]
            raw[12:16, at] = jnp.where(one, one1[c, b], one0[c, b])
            raw[16:20, at] = jnp.where(two, two1[c, b], two0[c, b])
    first = 4 * pos[1] - 6
    extent = 4 * ends[1]
    j = lax.broadcasted_iota(jnp.int32, (16, 24), 0)
    s = lax.broadcasted_iota(jnp.int32, (16, 24), 1)
    cell = mirror(first + j, extent)
    moved = jnp.where(s == cell - first + 2, 1.0, 0.0)
    raw[0:16] = matmul(moved, raw[...])
    row = lax.broadcasted_iota(jnp.int32, (16, LANES), 0) + first
    cross_sign = jnp.where((row < 0) | (row >= extent), -1.0, 1.0)
    begin = 2 * pos[0] - 6
    ax_extent = 2 * ends[0]
    origin = 2 * jnp.clip(pos[0] - 3, 0, ends[0] - 7)

    @pl.loop(0, 14, unroll=7)
    def _(r):
        g = begin + r
        at = mirror(g, ax_extent)
        sign = jnp.where(at == g, 1.0, -1.0)
        block = (at - origin) // 2
        half = (at - origin) % 2
        for c in range(5):
            x = raw[0:16, pl.ds(pl.multiple_of((c * 7 + block) * LANES, LANES), LANES)]
            x = jnp.where(half == 1, pltpu.roll(x, 64, 1), x)
            if c == 1:
                x = x * sign
            if c == 2:
                x = x * cross_sign
            v0[c, r, 0:16] = x

    level = Level(32, fields, carry, shift, matrix)
    chain(level, COARSE_PLAN, 16.0, 14, 16, v0, wa, wb, force, prim_v, prim_a, prim_b, rate, 32)
    lane = lax.broadcasted_iota(jnp.int32, (16, LANES), 1)
    sub = lax.broadcasted_iota(jnp.int32, (16, LANES), 0)
    valid = (lane < 32) & (sub >= 6) & (sub < 10)
    parts = []
    for c in range(5):
        for r in range(2):
            parts.append(jnp.where(valid, wb[c, 6 + r, 0:16] - v0[c, 6 + r, 0:16], 0.0))
    wide[...] = matmul(
        jnp.concatenate(parts, axis=0), pick((LANES, LANES), lambda a, b: a == b // 4)
    )
    parts = [diff[c, r] for c in range(5) for r in range(4)]
    tall[...] = matmul(
        jnp.concatenate(parts, axis=0), pick((LANES, LANES), lambda a, b: a == b // 2)
    )
    four = pick((16, 16), lambda a, b: b == 6 + a // 4)
    two = pick((16, 8), lambda a, b: b == a // 2)
    for c in range(5):
        for r in range(2):
            at = (c * 2 + r) * 16
            big = matmul(four, wide[at : at + 16])
            for m in range(2):
                at = (c * 4 + 2 * r + m) * 8
                step = big + matmul(two, tall[at : at + 8])
                for n in range(2):
                    row = 4 * r + 2 * m + n
                    out[c, row] = smoothed[c, row] + step


def coarse(ends, pos, own, neighbours, fields, diff, smoothed):
    scratch = [vmem(24, 35 * LANES)]
    cols = COARSE_COLS
    scratch += [vmem(5, 14, cols, LANES)] * 4 + [vmem(3, 14, cols, LANES)] * 3
    scratch += [vmem(14, cols, LANES), vmem(2, 12, 16, LANES), vmem(8, 12, 24, LANES), MATRIX]
    scratch += [vmem(160, LANES), vmem(160, LANES)]
    return call(
        functools.partial(coarse_kernel, ends),
        [smoothed.shape],
        scratch,
        20_000_000,
        pos,
        own,
        *neighbours,
        fields,
        diff,
        smoothed,
    )


def swapped(x, axis, by, phase):
    size = lax.axis_size(axis)
    low = [i for i in range(size - by) if (i // by) % 2 == phase]
    pairs = [(i, i + by) for i in low] + [(i + by, i) for i in low]
    return lax.ppermute(x, axis, sorted(pairs))


def wide_halos(own):
    a, x = odd(lax.axis_index("ax"), 1), odd(lax.axis_index("xs"), 1)
    ax1 = swapped(own, "ax", 1, 1)
    ax0 = swapped(own, "ax", 1, 0)

    def slab(phase):
        col = 8 * jnp.where(phase == 0, 1 - x, x)
        parts = [(ax0, 2 * a, 6), (own, 0, 8), (ax1, 2 * (1 - a), 6)]
        return jnp.concatenate(
            [lax.dynamic_slice(y, (0, row, col, 0), (5, n, 8, LANES)) for y, row, n in parts],
            axis=1,
        )

    xs1 = swapped(slab(1), "xs", 1, 1)
    xs0 = swapped(slab(0), "xs", 1, 0)
    return ax0, ax1, xs0, xs1


def wall_terms_kernel(factor, rows, count, origin, ends, pos, code, out, sides):
    extent = 8 * ends[0] // factor
    depth = 16 * ends[1] // factor
    scale = 1.0 / (factor * factor)
    begin = (8 // factor) * pos[0] - origin[0]
    first = (16 // factor) * pos[1] - origin[1]
    lane = lax.broadcasted_iota(jnp.int32, (count, LANES), 1)
    cell = mirror(lax.broadcasted_iota(jnp.int32, (count, LANES), 0) + first, depth)
    kinds = (1, 2, 0)

    def counts(r, kind, side):
        g = mirror(begin + r, extent)
        total = None
        for k in range(factor):
            hit = jnp.where(code[g * factor + k, side : side + 1] == kind, 1.0, 0.0)
            total = hit if total is None else total + hit
        return total

    if factor > 1:

        @pl.loop(0, rows, unroll=2)
        def _(r):
            for t, kind in enumerate(kinds):
                for side in range(2):
                    sides[pl.ds(r * 8 + 2 * t + side, 1)] = counts(r, kind, side)
            sides[pl.ds(r * 8 + 6, 2)] = jnp.zeros((2, LANES), jnp.float32)

        gather = pick((LANES, LANES), lambda a, b: a // factor == b)
        sides[...] = matmul(sides[...], gather)

    inside = cell == lane // factor

    @pl.loop(0, rows, unroll=2)
    def _(r):
        for t, kind in enumerate(kinds):
            edge = []
            for side in range(2):
                if factor > 1:
                    edge.append(sides[pl.ds(r * 8 + 2 * t + side, 1)])
                else:
                    edge.append(counts(r, kind, side))
            for side in (2, 3):
                line = jnp.broadcast_to(counts(r, kind, side), (count, LANES))
                edge.append(jnp.sum(jnp.where(inside, line, 0.0), axis=1, keepdims=True))
            total = jnp.where(cell == 0, edge[0], 0.0) + jnp.where(cell == depth - 1, edge[1], 0.0)
            total = total + jnp.where(lane == 0, edge[2], 0.0)
            total = total + jnp.where(lane == depth - 1, edge[3], 0.0)
            out[t, r] = scale * total


def wall_terms(ends, pos, code, factor, rows, count, origin):
    return call(
        functools.partial(wall_terms_kernel, factor, rows, count, origin, ends),
        [(3, rows, count, LANES)],
        [vmem(rows * 8, LANES)],
        1_000_000,
        pos,
        code,
    )


def per_device(state, wall_code):
    ends = (lax.axis_size("ax"), lax.axis_size("xs"))
    ax, xs = lax.axis_index("ax"), lax.axis_index("xs")
    pos = jnp.stack([ax, xs]).astype(jnp.int32)
    fine_fields = wall_terms(ends, pos, wall_code, 1, 24, FINE_COLS, (8, 8))
    middle_fields = wall_terms(ends, pos, wall_code, 2, 20, MIDDLE_COLS, (8, 8))
    coarse_fields = wall_terms(ends, pos, wall_code, 4, 14, COARSE_COLS, (6, 6))

    smoothed, *slabs = fine_relax(ends, pos, state, wide_halos(state), fine_fields, True)
    halos = [
        swapped(slab, axis, 1, phase)
        for slab, (axis, phase) in zip(slabs, (("ax", 0), ("ax", 1), ("xs", 0), ("xs", 1)))
    ]
    packed = fine_residual(ends, pos, smoothed, halos, fine_fields)

    two0, two1 = [swapped(packed, "ax", 2, phase) for phase in (0, 1)]
    one0, one1 = [swapped(packed, "ax", 1, phase) for phase in (0, 1)]
    b = odd(ax, 2)
    slab = jnp.concatenate(
        [
            lax.dynamic_slice_in_dim(two0, 2 * b, 2, axis=1),
            one0,
            packed,
            one1,
            lax.dynamic_slice_in_dim(two1, 2 * (1 - b), 2, axis=1),
        ],
        axis=1,
    )
    xs0, xs1 = [swapped(slab, "xs", 1, phase) for phase in (0, 1)]
    block, diff = middle(ends, pos, (two0, one0, packed, one1, two1), xs0, xs1, middle_fields)

    column = lax.all_to_all(block, "ax", 0, 0)
    start = jnp.clip(ax - 3, 0, ends[0] - 7)
    column = lax.dynamic_slice_in_dim(column, start, 7, axis=0)
    column = jnp.transpose(column, (1, 0, 2, 3))
    neighbours = [
        swapped(column, "xs", by, phase) for by, phase in ((2, 0), (1, 0), (1, 1), (2, 1))
    ]
    fine_new = coarse(ends, pos, column, neighbours, coarse_fields, diff, smoothed)

    return fine_relax(ends, pos, fine_new, wide_halos(fine_new), fine_fields, False)


def solution(mesh):
    in_specs = (P(None, "ax", "xs", None), P())
    out_specs = P(None, "ax", "xs", None)
    return jax.shard_map(
        per_device, mesh=mesh, in_specs=in_specs, out_specs=out_specs, check_vma=False
    )
```
